512 devices in a mesh: section: 4 (over x_hi, core), row: 128 (over z, x_lo, y).
Axes of the slice: x: 4 (x_hi: 2, x_lo: 2; x = x_hi * 2 + x_lo), y: 4, z: 16, core: 2. Of those that a mesh axis runs over, the one named last changes fastest.
Arguments:
- layer_input: bfloat16 [4, 16384, 4096], P('section', 'row'), may hold values from -6 to 6
- cotangent: bfloat16 [4, 16384, 4096], P('section', 'row'), may hold values from -6 to 6
- route_weight: float32 [4, 16384, 2], P('section', 'row'), may hold values from 0.1 to 0.9
- chosen: int32 [4, 16384, 2], P('section', 'row'), may hold values from 0 to 7, all different within a row
- hot_expert: int32 [4], P('section'), may hold values from 0 to 7
- store_in: bfloat16 [4, 2, 4096, 7168], P('section', None, None, 'row'), may hold values from -0.09375 to 0.09375
- store_out: bfloat16 [4, 7168, 4096], P('section', 'row'), may hold values from -0.0625 to 0.0625
Outputs:
- back_cot: bfloat16 [4, 16384, 4096], P('section', 'row')
- route_grad: float32 [4, 16384, 2], P('section', 'row')
The draws below stay inside these ranges and needn't reach their ends.
Inputs may be any that keep to these rules, and one draw needn't show every extreme that they name: `chosen`: each token names 2 different experts.
All inputs are finite; a program needn't handle non-finite values.
Results may differ from the reference program's by a relative error of at most 0.0034.
Values may be sent and summed in bfloat16 or wider, within the bound.
No kernel may reach another device: no remote copies, remote signals or barrier semaphores. Data moves between devices by JAX's collectives and lax.ppermute only.
A program may use at most 64 MiB of HBM per device.

```python
import jax
import jax.numpy as jnp
from jax import lax

D = 4096
FF = 7168
EXPERTS = 8
TOP = 2
TOK_DEV = 128
CAP = 2
SECTIONS = 4
TOKENS = 16384
N_ROW = 128


def plant(entries, stream_key, least, largest):
    place = [jax.random.randint(jax.random.fold_in(stream_key, axis), (), 0, length) for axis, length in enumerate(entries.shape)]
    widest = entries.shape.index(max(entries.shape))
    beside = place[:widest] + [(place[widest] + 1) % entries.shape[widest]] + place[widest + 1:]
    return entries.at[tuple(place)].set(least).at[tuple(beside)].set(largest)


def block_levels(rng, shape, pieces, smallest, high):
    factor_of = 1.0
    for axis_at, blocks in pieces:
        heights = jax.random.uniform(jax.random.fold_in(jax.random.fold_in(rng, 6), axis_at), (blocks,), jnp.float32, smallest / len(pieces), high / len(pieces))
        factor_of = factor_of * jnp.repeat(jnp.exp(heights), shape[axis_at] // blocks).reshape((-1,) + (1,) * (len(shape) - 1 - axis_at))
    return factor_of


def picks_of(key, rows, amount, top, lift):
    ranking = jax.random.permutation(jax.random.fold_in(key, 1), amount)
    favour = ranking
    for power in range(3):
        favour = favour * favour // amount
    favour = favour * lift // amount
    lots = jax.random.randint(jax.random.fold_in(key, 2), (rows, amount), 0, 4096) + favour
    fixed_rows = jax.random.permutation(jax.random.fold_in(key, 3), rows)[jnp.arange(amount) % rows]
    lots = jnp.where(jnp.arange(rows)[:, None] == fixed_rows[None, :], 1 << 14, lots)
    score = lots * amount + jnp.arange(amount)
    return lax.top_k(score.astype(jnp.int32), top)[1].astype(jnp.int32)


def scatter_about(key, dims, deviation, reach, pieces=(), kind=jnp.bfloat16):
    result = deviation * jax.random.normal(key, dims, jnp.float32)
    if pieces:
        result = result * block_levels(key, dims, pieces, -0.22, 0.18)
    return jnp.clip(result, -reach, reach).astype(kind)


def setup_inputs(seed: int = 0) -> dict:
    streams_of = jax.random.split(jax.random.key(seed), 8)
    layer_input = scatter_about(streams_of[0], (SECTIONS, TOKENS, D), 1.0, 6.0, ((0, 4), (1, 128)))
    cotangent = scatter_about(streams_of[1], (SECTIONS, TOKENS, D), 1.0, 6.0, ((0, 4), (1, 128)))
    route_weight = jnp.clip(0.1 + 0.79999997 * jax.random.uniform(streams_of[2], (SECTIONS, TOKENS, TOP), jnp.float32) ** block_levels(streams_of[2], (SECTIONS, TOKENS, TOP), ((0, 4), (1, 128)), -0.2, 0.2), 0.1, 0.9)
    chosen = picks_of(streams_of[3], SECTIONS * TOKENS, EXPERTS, TOP, 4096).reshape((SECTIONS, TOKENS, TOP))
    hot_expert = plant(jax.random.randint(streams_of[4], (SECTIONS,), 0, EXPERTS), jax.random.fold_in(streams_of[4], 1), 0, EXPERTS - 1).astype(jnp.int32)
    store_in = scatter_about(streams_of[5], (SECTIONS, 2, D, FF), D ** -0.5, 0.09375, ((0, 4), (3, 128)))
    store_out = scatter_about(streams_of[6], (SECTIONS, FF, D), FF ** -0.5, 0.0625, ((0, 4), (1, 128)))
    return dict(layer_input=layer_input, cotangent=cotangent, route_weight=route_weight, chosen=chosen, hot_expert=hot_expert, store_in=store_in, store_out=store_out)


def token_select(block_c, hot):
    hit = (block_c == hot).astype(jnp.int32).reshape(-1)
    order = (jnp.cumsum(hit) - hit).astype(jnp.int32)
    held = (hit * (order < CAP).astype(jnp.int32)).astype(jnp.int32)
    slots = (order[None, :] == jnp.arange(CAP, dtype=jnp.int32)[:, None]).astype(jnp.int32) * held[None, :]
    tsel = jnp.sum(slots.reshape(CAP, TOK_DEV, TOP), axis=2).astype(jnp.int32)
    return tsel, held.reshape(TOK_DEV, TOP)


def reference(layer_input, cotangent, route_weight, chosen, hot_expert, store_in, store_out):
    high = lax.Precision.HIGHEST
    moved_all = []
    grad_all = []
    for section in range(SECTIONS):
        hot = hot_expert[section]
        blocks_x = layer_input[section].reshape(N_ROW, TOK_DEV, D)
        blocks_g = cotangent[section].reshape(N_ROW, TOK_DEV, D)
        blocks_w = route_weight[section].reshape(N_ROW, TOK_DEV, TOP)
        blocks_c = chosen[section].reshape(N_ROW, TOK_DEV, TOP)

        def build(items):
            tsel, held = token_select(items[2], hot)
            pick = tsel.astype(jnp.float32)
            rx = jnp.dot(pick, items[0].astype(jnp.float32), precision=high).astype(jnp.bfloat16)
            rg = jnp.dot(pick, items[1].astype(jnp.float32), precision=high).astype(jnp.bfloat16)
            return rx, rg

        rows_x, rows_g = lax.map(build, (blocks_x, blocks_g, blocks_c))
        rows_x = rows_x.reshape(N_ROW * CAP, D).astype(jnp.float32)
        rows_g = rows_g.reshape(N_ROW * CAP, D).astype(jnp.float32)
        w_gate = store_in[section, 0].astype(jnp.float32)
        w_up = store_in[section, 1].astype(jnp.float32)
        w_out = store_out[section].astype(jnp.float32)
        gate = jnp.dot(rows_x, w_gate, precision=high)
        upper = jnp.dot(rows_x, w_up, precision=high)
        sig = jax.nn.sigmoid(gate)
        hidden = (gate * sig * upper).astype(jnp.bfloat16)
        out = jnp.dot(hidden.astype(jnp.float32), w_out, precision=high)
        d_hidden = jnp.dot(rows_g, w_out.T, precision=high)
        d_gate = (d_hidden * upper * sig * (1.0 + gate * (1.0 - sig))).astype(jnp.bfloat16)
        d_up = (d_hidden * gate * sig).astype(jnp.bfloat16)
        back = (jnp.dot(d_gate.astype(jnp.float32), w_gate.T, precision=high) + jnp.dot(d_up.astype(jnp.float32), w_up.T, precision=high)).astype(jnp.bfloat16)
        out_blocks = out.reshape(N_ROW, CAP, D)
        back_blocks = back.reshape(N_ROW, CAP, D)

        def finish(items):
            block_g, block_w, block_c, out_b, back_b = items
            tsel, held = token_select(block_c, hot)
            pick = tsel.astype(jnp.float32)
            out_tok = jnp.dot(pick.T, out_b, precision=high)
            back_tok = jnp.dot(pick.T, back_b.astype(jnp.float32), precision=high)
            weight_tok = jnp.sum(held.astype(jnp.float32) * block_w, axis=1)
            cot = block_g.astype(jnp.float32)
            moved = (cot + weight_tok[:, None] * back_tok).astype(jnp.bfloat16)
            grad = held.astype(jnp.float32) * jnp.sum(cot * out_tok, axis=1)[:, None]
            return moved, grad

        moved, grad = lax.map(finish, (blocks_g, blocks_w, blocks_c, out_blocks, back_blocks))
        moved_all.append(moved.reshape(TOKENS, D))
        grad_all.append(grad.reshape(TOKENS, TOP))
    zeros = jnp.zeros((TOKENS, D), jnp.bfloat16)
    back_cot = jnp.stack(moved_all[1:] + [zeros], axis=0)
    return back_cot, jnp.stack(grad_all, axis=0)
```

```python
import jax
import jax.numpy as jnp
from jax import lax
from jax.experimental import pallas as pl
from jax.experimental.pallas import tpu as pltpu
from jax.sharding import PartitionSpec as P

CAP = 2
PLANE = 8
SENT_DOWN = 32
PAD = 128
NONE = 128

bf16 = jnp.bfloat16
f32 = jnp.float32


def slot_tokens(chosen_ref, hot_ref):
    hit = chosen_ref[...] == hot_ref[0]
    lane = lax.broadcasted_iota(jnp.int32, hit.shape, 1)
    at = jnp.where(hit, lane, NONE)
    first = jnp.min(jnp.min(at, axis=1, keepdims=True), axis=0, keepdims=True)
    later = jnp.where(at > first, at, NONE)
    second = jnp.min(jnp.min(later, axis=1, keepdims=True), axis=0, keepdims=True)
    return hit, lane, first, second


def total(values):
    return jnp.sum(jnp.sum(values, axis=1, keepdims=True), axis=0, keepdims=True)


def select_kernel(chosen_ref, hot_ref, weight_ref, x_ref, g_ref, sent_ref, cot_ref, w_ref, t_ref):
    hit, lane, first, second = slot_tokens(chosen_ref, hot_ref)
    weights = weight_ref[...]
    w_first = total(jnp.where(hit & (lane == first), weights, 0.0))
    w_second = total(jnp.where(hit & (lane == second), weights, 0.0))
    tokens = x_ref.shape[0]
    row = lax.broadcasted_iota(jnp.int32, (8, tokens), 0)
    col = lax.broadcasted_iota(jnp.int32, (8, tokens), 1)
    token = jnp.where(row < 4, first, second)
    pick = (col == token).astype(f32).astype(bf16)
    t_ref[...] = token.astype(f32)
    w_ref[...] = jnp.where(row < 4, w_first, w_second)
    x_rows = jnp.dot(pick, x_ref[...], preferred_element_type=f32)
    g_rows = jnp.dot(pick, g_ref[...], preferred_element_type=f32)
    half = x_rows.shape[1] // 2
    quarter = half // 2
    at = lax.broadcasted_iota(jnp.int32, (8, half), 0)
    low = (at & 2) == 0
    unit = jnp.where(
        (at & 1) == 0,
        jnp.where(low, x_rows[:, :half], x_rows[:, half:]),
        jnp.where(low, g_rows[:, :half], g_rows[:, half:]),
    ).astype(bf16)
    for i in range(sent_ref.shape[0]):
        sent_ref[i] = unit
    at = lax.broadcasted_iota(jnp.int32, (8, quarter), 0) & 3
    cot = g_rows[:, :quarter]
    for q in range(1, 4):
        cot = jnp.where(at == q, g_rows[:, q * quarter : (q + 1) * quarter], cot)
    cot_ref[...] = cot


def expert_kernel(rows_ref, in_ref, out_ref, below_ref, above_ref, part_ref, w_all, prod, wide):
    width = in_ref.shape[2]
    half, quarter = width // 2, width // 4
    count = rows_ref.shape[0] // 4
    own = in_ref.shape[1]
    n_above, n_below = above_ref.shape[1], below_ref.shape[1]
    for kind in range(3):
        at = kind * PAD
        w_all[at + 48 : at + 64, :] = jnp.zeros((16, width), bf16)
        w_all[at + 112 : at + 128, :] = jnp.zeros((16, width), bf16)
        w_all[at : at + n_above, :] = above_ref[kind]
        w_all[at + n_above : at + n_above + n_below, :] = below_ref[kind]
        w_all[at + 64 : at + 64 + own, :] = in_ref[kind] if kind < 2 else out_ref[...]
    nt = (((1,), (1,)), ((), ()))
    for h in range(2):
        out = lax.dot_general(
            rows_ref[...], w_all[:, h * half : (h + 1) * half], nt, preferred_element_type=f32
        )
        for column in range(3):
            prod[h * 3 + column] = out[:, column * PAD : (column + 1) * PAD]

    def taken(kind, column):
        low = prod[column, pl.ds(kind, count, stride=4), :]
        return low + prod[3 + column, pl.ds(2 + kind, count, stride=4), :]

    gate, upper, d_hidden = taken(0, 0), taken(0, 1), taken(1, 2)
    sig = 1.0 / (1.0 + jnp.exp(-gate))
    hidden = (gate * sig * upper).astype(bf16)
    d_gate = (d_hidden * upper * sig * (1.0 + gate * (1.0 - sig))).astype(bf16)
    d_up = (d_hidden * gate * sig).astype(bf16)
    score = jnp.sum(hidden.astype(f32) * d_hidden, axis=1, keepdims=True)
    both = jnp.concatenate([d_gate, d_up], axis=1)
    for q in range(4):
        cols = slice(q * quarter, (q + 1) * quarter)
        back = jnp.dot(both, w_all[: 2 * PAD, cols], preferred_element_type=f32)
        for i in range(quarter // 128):
            wide[i, pl.ds(q, count, stride=4), :] = back[:, i * 128 : (i + 1) * 128]
    split_score(wide, quarter // 128, jnp.broadcast_to(score, (count, 128)))
    for i in range(quarter // 128 + 1):
        part_ref[:, i * 128 : (i + 1) * 128] = wide[i].astype(bf16)


def split_score(wide, at, score):
    count = score.shape[0]
    for q in range(3):
        piece = score.astype(bf16).astype(f32)
        wide[at, pl.ds(q, count, stride=4), :] = piece
        score = score - piece
    wide[at, pl.ds(3, count, stride=4), :] = jnp.zeros_like(score)


def joined_score(wide, at, count):
    pieces = [wide[at, pl.ds(q, count, stride=4), :] for q in range(3)]
    return pieces[2] + pieces[1] + pieces[0]


def summed(got_ref):
    acc = got_ref[0].astype(f32)
    for i in range(1, got_ref.shape[0]):
        acc = acc + got_ref[i].astype(f32)
    return acc


def middle_kernel(got_ref, part_ref, wide):
    acc = summed(got_ref)
    at = acc.shape[1] - 128
    wide[0] = acc[:, at:]
    split_score(wide, 0, joined_score(wide, 0, acc.shape[0] // 4))
    part_ref[:, :at] = acc[:, :at].astype(bf16)
    part_ref[:, at:] = wide[0].astype(bf16)


def last_kernel(got_ref, cot_ref, w_ref, t_ref, chosen_ref, hot_ref, moved_ref, grad_ref, wide):
    acc = summed(got_ref)
    quarter = cot_ref.shape[1]
    wide[0] = acc[:, quarter:]
    back = acc[:, :quarter].astype(bf16).astype(f32)
    w = w_ref[:, :1]
    moved_ref[:, :quarter] = (cot_ref[...] + w * back).astype(bf16)
    moved_ref[:, quarter:] = t_ref[...].astype(bf16)
    score = joined_score(wide, 0, 2)
    hit, lane, first, second = slot_tokens(chosen_ref, hot_ref)
    grad = jnp.where(lane == first, score[0:1], jnp.where(lane == second, score[1:2], 0.0))
    grad_ref[...] = jnp.where(hit, grad, 0.0)


def place_kernel(cot_ref, moved_ref, out_ref):
    tokens, width = cot_ref.shape
    quarter = width // 4
    row = lax.broadcasted_iota(jnp.int32, (tokens, 128), 0).astype(f32)
    token = moved_ref[:, quarter:].astype(f32)
    at = [(row == token[4 * s : 4 * s + 1])[:, :1] for s in range(CAP)]
    for q in range(4):
        cols = slice(q * quarter, (q + 1) * quarter)
        value = cot_ref[:, cols].astype(f32)
        for s in range(CAP):
            value = jnp.where(at[s], moved_ref[4 * s + q : 4 * s + q + 1, :quarter].astype(f32), value)
        out_ref[:, cols] = value.astype(bf16)


def call(kernel, outs, *operands, scratch=(), smem=()):
    specs = [
        pl.BlockSpec(memory_space=pltpu.SMEM if i in smem else pltpu.VMEM) for i in range(len(operands))
    ]
    many = isinstance(outs, (list, tuple))
    return pl.pallas_call(
        kernel,
        out_shape=outs,
        in_specs=specs,
        out_specs=[pl.BlockSpec(memory_space=pltpu.VMEM)] * len(outs) if many else pl.BlockSpec(memory_space=pltpu.VMEM),
        scratch_shapes=list(scratch),
    )(*operands)


def shape(dims, kind):
    return jax.ShapeDtypeStruct(dims, kind)


def on_device(layer_input, cotangent, route_weight, chosen, hot_expert, store_in, store_out):
    tokens, width = layer_input.shape[1:]
    half, quarter = width // 2, width // 4
    num_row = lax.axis_size("row")
    heights = num_row // PLANE
    peers = heights // 2
    along_z = [[a * 2 * PLANE + r for a in range(peers)] for r in range(2 * PLANE)]
    in_plane = [[z * PLANE + i for i in range(PLANE)] for z in range(heights)]
    sections = lax.axis_size("section")
    back_one = [(i, i - 1) for i in range(1, sections)]

    def exchange(value, groups):
        return lax.all_to_all(
            value, "row", split_axis=0, concat_axis=0, axis_index_groups=groups, tiled=True
        )

    def along(value, by):
        return lax.ppermute(value, "row", [(i, (i + by * PLANE) % num_row) for i in range(num_row)])

    w_in = jnp.swapaxes(store_in[0], 1, 2)
    w_out = store_out[0]
    w_both = jnp.concatenate([w_in, w_out[None]], axis=0)
    from_above = along(w_both[:, :SENT_DOWN], -1)
    from_below = along(w_both[:, SENT_DOWN:], 1)
    cot_moved = lax.ppermute(cotangent[0], "section", back_one)

    chosen_t = chosen[0].T
    unit, cot_rows, w_rows, t_rows = call(
        select_kernel,
        [
            shape((peers, 8, half), bf16),
            shape((8, quarter), f32),
            shape((8, tokens), f32),
            shape((8, tokens), f32),
        ],
        chosen_t,
        hot_expert,
        route_weight[0].T,
        layer_input[0],
        cotangent[0],
        smem=(1,),
    )
    column = exchange(unit, along_z).reshape(peers * 8, half)
    rows = exchange(jnp.broadcast_to(column[None], (PLANE, peers * 8, half)), in_plane)
    wide = quarter + 128
    count = PLANE * peers * 8
    part = call(
        expert_kernel,
        shape((count, wide), bf16),
        rows.reshape(count, half),
        w_in,
        w_out,
        from_below,
        from_above,
        scratch=(
            pltpu.VMEM((3 * PAD, width), bf16),
            pltpu.VMEM((6, count, PAD), f32),
            pltpu.VMEM((wide // 128, count, 128), f32),
        ),
    )
    got = exchange(part.reshape(PLANE, peers * 8, wide), in_plane)
    part = call(
        middle_kernel, shape((peers * 8, wide), bf16), got, scratch=(pltpu.VMEM((1, peers * 8, 128), f32),)
    )
    got = exchange(part.reshape(peers, 8, wide), along_z)
    moved, grad = call(
        last_kernel,
        [shape((8, wide), bf16), shape((2, tokens), f32)],
        got,
        cot_rows,
        w_rows,
        t_rows,
        chosen_t,
        hot_expert,
        scratch=(pltpu.VMEM((1, 8, 128), f32),),
        smem=(5,),
    )
    moved = lax.ppermute(moved, "section", back_one)
    back_cot = call(place_kernel, shape((tokens, width), bf16), cot_moved, moved)
    return (back_cot[None], grad.T[None])


def solution(mesh):
    in_specs = (
        P("section", "row", None),
        P("section", "row", None),
        P("section", "row", None),
        P("section", "row", None),
        P("section"),
        P("section", None, None, "row"),
        P("section", "row", None),
    )
    out_specs = (P("section", "row", None), P("section", "row", None))
    return jax.shard_map(
        on_device, mesh=mesh, in_specs=in_specs, out_specs=out_specs, check_vma=False
    )
```

```python
import jax
import jax.numpy as jnp
from jax import lax
from jax.experimental import pallas as pl
from jax.experimental.pallas import tpu as pltpu
from jax.sharding import PartitionSpec as P

CAP = 2
TOP = 2
PLANE = 8
SENT_DOWN = 32
PAD = 128
NONE = 128

bf16 = jnp.bfloat16
f32 = jnp.float32


def slot_tokens(chosen, hot):
    hit = chosen == hot
    lane = lax.broadcasted_iota(jnp.int32, hit.shape, 1)
    at = jnp.where(hit, lane, NONE)
    first = jnp.min(jnp.min(at, axis=1, keepdims=True), axis=0, keepdims=True)
    later = jnp.where(at > first, at, NONE)
    second = jnp.min(jnp.min(later, axis=1, keepdims=True), axis=0, keepdims=True)
    return hit, lane, first, second


def total(values):
    return jnp.sum(jnp.sum(values, axis=1, keepdims=True), axis=0, keepdims=True)


def select_kernel(
    chosen_hbm, hot_ref, weight_hbm, x_hbm, g_hbm,
    sent_ref, cot_ref, w_ref, t_ref, held_ref,
    chosen_ref, weight_ref, x_ref, g_ref, sems,
):
    pairs = (
        (chosen_hbm, chosen_ref),
        (weight_hbm, weight_ref),
        (x_hbm, x_ref),
        (g_hbm, g_ref),
    )
    coming = [pltpu.make_async_copy(src, dst, sems.at[i]) for i, (src, dst) in enumerate(pairs)]
    for copy in coming:
        copy.start()
    for copy in coming[:2]:
        copy.wait()
    hit, lane, first, second = slot_tokens(chosen_ref[...], hot_ref[0])
    weights = weight_ref[...]
    in_first, in_second = hit & (lane == first), hit & (lane == second)
    held_ref[...] = jnp.zeros_like(held_ref)
    held_ref[0:2] = in_first.astype(f32)
    held_ref[4:6] = in_second.astype(f32)
    w_first = total(jnp.where(in_first, weights, 0.0))
    w_second = total(jnp.where(in_second, weights, 0.0))
    tokens = x_ref.shape[0]
    row = lax.broadcasted_iota(jnp.int32, (8, tokens), 0)
    col = lax.broadcasted_iota(jnp.int32, (8, tokens), 1)
    token = jnp.where(row < 4, first, second)
    pick = (col == token).astype(f32).astype(bf16)
    t_ref[...] = token.astype(f32)
    w_ref[...] = jnp.where(row < 4, w_first, w_second)
    for copy in coming[2:]:
        copy.wait()
    x_rows = jnp.dot(pick, x_ref[...], preferred_element_type=f32)
    g_rows = jnp.dot(pick, g_ref[...], preferred_element_type=f32)
    half = x_rows.shape[1] // 2
    quarter = half // 2
    at = lax.broadcasted_iota(jnp.int32, (8, half), 0)
    low = (at & 2) == 0
    unit = jnp.where(
        (at & 1) == 0,
        jnp.where(low, x_rows[:, :half], x_rows[:, half:]),
        jnp.where(low, g_rows[:, :half], g_rows[:, half:]),
    ).astype(bf16)
    for i in range(sent_ref.shape[0]):
        sent_ref[i] = unit
    at = lax.broadcasted_iota(jnp.int32, (8, quarter), 0) & 3
    cot = g_rows[:, :quarter]
    for q in range(1, 4):
        cot = jnp.where(at == q, g_rows[:, q * quarter : (q + 1) * quarter], cot)
    cot_ref[...] = cot


def weights_kernel(in_ref, out_ref, below_ref, above_ref, w_all):
    width, own = in_ref.shape[2], in_ref.shape[1]
    n_above, n_below = above_ref.shape[1], below_ref.shape[1]
    for kind in range(3):
        at = kind * PAD
        w_all[at + 48 : at + 64, :] = jnp.zeros((16, width), bf16)
        w_all[at + 112 : at + 128, :] = jnp.zeros((16, width), bf16)
        w_all[at : at + n_above, :] = above_ref[kind]
        w_all[at + n_above : at + n_above + n_below, :] = below_ref[kind]
        w_all[at + 64 : at + 64 + own, :] = in_ref[kind] if kind < 2 else out_ref[...]


def spread_kernel(column_ref, sent_ref, sems):
    copies = [
        pltpu.make_async_copy(column_ref, sent_ref.at[i], sems.at[i]) for i in range(sent_ref.shape[0])
    ]
    for copy in copies:
        copy.start()
    for copy in copies:
        copy.wait()


def expert_kernel(rows_hbm, w_all, part_hbm, rows_ref, prod, wide, part_ref, in_sems, out_sems):
    width = w_all.shape[1]
    half, quarter = width // 2, width // 4
    tall = rows_ref.shape[0]
    count = tall // 4
    pieces = in_sems.shape[0]
    height = tall // pieces
    coming = []
    for i in range(pieces):
        at = slice(i * height, (i + 1) * height)
        coming.append(pltpu.make_async_copy(rows_hbm.at[at], rows_ref.at[at], in_sems.at[i]))
        coming[i].start()
    nt = (((1,), (1,)), ((), ()))
    for i in range(pieces):
        at = slice(i * height, (i + 1) * height)
        coming[i].wait()
        for h in range(2):
            cols = slice(h * half, (h + 1) * half)
            out = lax.dot_general(
                rows_ref[at, :],
                w_all[:, cols],
                nt,
                preferred_element_type=f32,
            )
            for column in range(3):
                prod[h * 3 + column, at, :] = out[:, column * PAD : (column + 1) * PAD]

    def taken(kind, column):
        low = prod[column, pl.ds(kind, count, stride=4), :]
        return low + prod[3 + column, pl.ds(2 + kind, count, stride=4), :]

    gate, upper, d_hidden = taken(0, 0), taken(0, 1), taken(1, 2)
    sig = 1.0 / (1.0 + jnp.exp(-gate))
    hidden = (gate * sig * upper).astype(bf16)
    d_gate = (d_hidden * upper * sig * (1.0 + gate * (1.0 - sig))).astype(bf16)
    d_up = (d_hidden * gate * sig).astype(bf16)
    score = jnp.sum(hidden.astype(f32) * d_hidden, axis=1, keepdims=True)
    both = jnp.concatenate([d_gate, d_up], axis=1)
    blocks = quarter // 128
    going = []

    def send(at, blocks_there):
        for i in range(at, at + blocks_there):
            part_ref[:, i * 128 : (i + 1) * 128] = wide[i].astype(bf16)
        cols = slice(at * 128, (at + blocks_there) * 128)
        copy = pltpu.make_async_copy(part_ref.at[:, cols], part_hbm.at[:, cols], out_sems.at[len(going)])
        copy.start()
        going.append(copy)

    split_score(wide, blocks, jnp.broadcast_to(score, (count, 128)))
    send(blocks, 1)
    for at in range(0, blocks, 2):
        for q in range(4):
            cols = slice(q * quarter + at * 128, q * quarter + (at + 2) * 128)
            back = jnp.dot(both, w_all[: 2 * PAD, cols], preferred_element_type=f32)
            wide[at, pl.ds(q, count, stride=4), :] = back[:, :128]
            wide[at + 1, pl.ds(q, count, stride=4), :] = back[:, 128:]
        send(at, 2)
    for copy in going:
        copy.wait()


def split_score(wide, at, score):
    count = score.shape[0]
    for q in range(3):
        piece = score.astype(bf16).astype(f32)
        wide[at, pl.ds(q, count, stride=4), :] = piece
        score = score - piece
    wide[at, pl.ds(3, count, stride=4), :] = jnp.zeros_like(score)


def joined_score(wide, at, count):
    pieces = [wide[at, pl.ds(q, count, stride=4), :] for q in range(3)]
    return pieces[2] + pieces[1] + pieces[0]


def summed(got_ref):
    acc = got_ref[0].astype(f32)
    for i in range(1, got_ref.shape[0]):
        acc = acc + got_ref[i].astype(f32)
    return acc


def middle_kernel(got_ref, part_ref, wide):
    acc = summed(got_ref)
    at = acc.shape[1] - 128
    wide[0] = acc[:, at:]
    split_score(wide, 0, joined_score(wide, 0, acc.shape[0] // 4))
    part_ref[:, :at] = acc[:, :at].astype(bf16)
    part_ref[:, at:] = wide[0].astype(bf16)


def last_kernel(got_ref, cot_ref, w_ref, t_ref, held_ref, moved_ref, grad_ref, wide):
    acc = summed(got_ref)
    quarter = cot_ref.shape[1]
    wide[0] = acc[:, quarter:]
    back = acc[:, :quarter].astype(bf16).astype(f32)
    w = w_ref[:, :1]
    moved_ref[:, :quarter] = (cot_ref[...] + w * back).astype(bf16)
    moved_ref[:, quarter:] = t_ref[...].astype(bf16)
    score = joined_score(wide, 0, 2)
    grad_ref[...] = held_ref[0:2] * score[0:1] + held_ref[4:6] * score[1:2]


def place_kernel(cot_ref, moved_ref, out_ref, ready, sems):
    tokens, width = cot_ref.shape
    quarter = width // 4
    row = lax.broadcasted_iota(jnp.int32, (tokens, 128), 0).astype(f32)
    token = moved_ref[:, quarter:].astype(f32)
    at = [(row == token[4 * s : 4 * s + 1])[:, :1] for s in range(CAP)]
    copies = []
    for q in range(4):
        cols = slice(q * quarter, (q + 1) * quarter)
        value = cot_ref[:, cols].astype(f32)
        for s in range(CAP):
            value = jnp.where(at[s], moved_ref[4 * s + q : 4 * s + q + 1, :quarter].astype(f32), value)
        ready[:, cols] = value.astype(bf16)
        copies.append(pltpu.make_async_copy(ready.at[:, cols], out_ref.at[:, cols], sems.at[q]))
        copies[q].start()
    for copy in copies:
        copy.wait()


def call(kernel, outs, *operands, scratch=(), smem=(), near=(), far=(), out_space=pltpu.VMEM):
    def placed(i, v):
        if i in near or i in far:
            return pltpu.with_memory_space_constraint(v, pltpu.VMEM if i in near else pltpu.HBM)
        return v

    def space(i):
        return pltpu.SMEM if i in smem else pltpu.HBM if i in far else pltpu.VMEM

    return pl.pallas_call(
        kernel,
        out_shape=outs,
        in_specs=[pl.BlockSpec(memory_space=space(i)) for i in range(len(operands))],
        out_specs=[pl.BlockSpec(memory_space=out_space)] * len(outs),
        scratch_shapes=list(scratch),
        compiler_params=pltpu.CompilerParams(vmem_limit_bytes=24 << 20),
    )(*(placed(i, v) for i, v in enumerate(operands)))


def shape(dims, kind):
    return jax.ShapeDtypeStruct(dims, kind)


def on_device(layer_input, cotangent, route_weight, chosen, hot_expert, store_in, store_out):
    tokens, width = layer_input.shape[1:]
    half, quarter = width // 2, width // 4
    num_row = lax.axis_size("row")
    heights = num_row // PLANE
    peers = heights // 2
    along_z = [[a * 2 * PLANE + r for a in range(peers)] for r in range(2 * PLANE)]
    in_plane = [[z * PLANE + i for i in range(PLANE)] for z in range(heights)]
    sections = lax.axis_size("section")
    back_one = [(i, i - 1) for i in range(1, sections)]

    def exchange(value, groups):
        return lax.all_to_all(
            value, "row", split_axis=0, concat_axis=0, axis_index_groups=groups, tiled=True
        )

    def along(value, by):
        return lax.ppermute(value, "row", [(i, (i + by * PLANE) % num_row) for i in range(num_row)])

    w_in = jnp.swapaxes(store_in[0], 1, 2)
    w_out = store_out[0]
    w_both = jnp.concatenate([w_in, w_out[None]], axis=0)
    from_above = along(w_both[:, :SENT_DOWN], -1)
    from_below = along(w_both[:, SENT_DOWN:], 1)
    cot_moved = lax.ppermute(cotangent[0], "section", back_one)

    unit, cot_rows, w_rows, t_rows, held = call(
        select_kernel,
        [
            pltpu.VMEM((peers, 8, half), bf16),
            pltpu.VMEM((8, quarter), f32),
            pltpu.VMEM((8, tokens), f32),
            pltpu.VMEM((8, tokens), f32),
            pltpu.VMEM((8, tokens), f32),
        ],
        chosen[0].T,
        hot_expert,
        route_weight[0].T,
        layer_input[0],
        cotangent[0],
        scratch=(
            pltpu.VMEM((TOP, tokens), jnp.int32),
            pltpu.VMEM((TOP, tokens), f32),
            pltpu.VMEM((tokens, width), bf16),
            pltpu.VMEM((tokens, width), bf16),
            pltpu.SemaphoreType.DMA((4,)),
        ),
        smem=(1,),
        far=(0, 2, 3, 4),
    )
    tall = peers * 8
    column = exchange(unit, along_z).reshape(tall, half)
    (sent,) = call(
        spread_kernel,
        [pltpu.HBM((PLANE, tall, half), bf16)],
        column,
        scratch=(pltpu.SemaphoreType.DMA((PLANE,)),),
        near=(0,),
        out_space=pltpu.HBM,
    )
    rows = exchange(sent, in_plane)
    (w_all,) = call(
        weights_kernel, [pltpu.VMEM((3 * PAD, width), bf16)], w_in, w_out, from_below, from_above, near=(0, 1, 2, 3)
    )
    wide = quarter + 128
    count = PLANE * tall
    (part,) = call(
        expert_kernel,
        [pltpu.HBM((count, wide), bf16)],
        rows.reshape(count, half),
        w_all,
        scratch=(
            pltpu.VMEM((count, half), bf16),
            pltpu.VMEM((6, count, PAD), f32),
            pltpu.VMEM((wide // 128, count, 128), f32),
            pltpu.VMEM((count, wide), bf16),
            pltpu.SemaphoreType.DMA((2,)),
            pltpu.SemaphoreType.DMA((5,)),
        ),
        near=(1,),
        far=(0,),
        out_space=pltpu.HBM,
    )
    got = exchange(part.reshape(PLANE, tall, wide), in_plane)
    (part,) = call(
        middle_kernel,
        [pltpu.VMEM((tall, wide), bf16)],
        got,
        scratch=(pltpu.VMEM((1, tall, 128), f32),),
        near=(0,),
    )
    got = exchange(part.reshape(peers, 8, wide), along_z)
    moved, grad = call(
        last_kernel,
        [pltpu.VMEM((8, wide), bf16), shape((2, tokens), f32)],
        got,
        cot_rows,
        w_rows,
        t_rows,
        held,
        scratch=(pltpu.VMEM((1, 8, 128), f32),),
        near=(0, 1, 2, 3, 4),
    )
    moved = lax.ppermute(moved, "section", back_one)
    (back_cot,) = call(
        place_kernel,
        [pltpu.HBM((tokens, width), bf16)],
        cot_moved,
        moved,
        scratch=(pltpu.VMEM((tokens, width), bf16), pltpu.SemaphoreType.DMA((4,))),
        near=(0, 1),
        out_space=pltpu.HBM,
    )
    return (back_cot[None], grad.T[None])


def solution(mesh):
    in_specs = (
        P("section", "row", None),
        P("section", "row", None),
        P("section", "row", None),
        P("section", "row", None),
        P("section"),
        P("section", None, None, "row"),
        P("section", "row", None),
    )
    out_specs = (P("section", "row", None), P("section", "row", None))
    return jax.shard_map(
        on_device, mesh=mesh, in_specs=in_specs, out_specs=out_specs, check_vma=False
    )
```

```python
import jax
import jax.numpy as jnp
from jax import lax
from jax.experimental import pallas as pl
from jax.experimental.pallas import tpu as pltpu
from jax.sharding import PartitionSpec as P


CAP = 2
TOP = 2
PLANE = 8
PAD = 128
NONE = 128

bf16 = jnp.bfloat16
f32 = jnp.float32


def slot_tokens(chosen, hot):
    hit = chosen == hot
    lane = lax.broadcasted_iota(jnp.int32, hit.shape, 1)
    at = jnp.where(hit, lane, NONE)
    first = jnp.min(jnp.min(at, axis=1, keepdims=True), axis=0, keepdims=True)
    later = jnp.where(at > first, at, NONE)
    second = jnp.min(jnp.min(later, axis=1, keepdims=True), axis=0, keepdims=True)
    return hit, lane, first, second


def total(values):
    return jnp.sum(jnp.sum(values, axis=1, keepdims=True), axis=0, keepdims=True)


def select_kernel(
    chosen_hbm, hot_ref, weight_hbm, x_hbm, g_hbm,
    sent_ref, cot_ref, w_ref, t_ref, held_ref,
    chosen_ref, weight_ref, x_ref, g_ref, sems,
):
    pairs = (
        (chosen_hbm, chosen_ref),
        (weight_hbm, weight_ref),
        (x_hbm, x_ref),
        (g_hbm, g_ref),
    )
    coming = [pltpu.make_async_copy(src, dst, sems.at[i]) for i, (src, dst) in enumerate(pairs)]
    for copy in coming:
        copy.start()
    for copy in coming[:2]:
        copy.wait()
    hit, lane, first, second = slot_tokens(chosen_ref[...], hot_ref[0])
    weights = weight_ref[...]
    in_first, in_second = hit & (lane == first), hit & (lane == second)
    held_ref[...] = jnp.zeros_like(held_ref)
    held_ref[0:2] = in_first.astype(f32)
    held_ref[4:6] = in_second.astype(f32)
    w_first = total(jnp.where(in_first, weights, 0.0))
    w_second = total(jnp.where(in_second, weights, 0.0))
    tokens = x_ref.shape[0]
    row = lax.broadcasted_iota(jnp.int32, (8, tokens), 0)
    col = lax.broadcasted_iota(jnp.int32, (8, tokens), 1)
    token = jnp.where(row < 4, first, second)
    pick = (col == token).astype(f32).astype(bf16)
    t_ref[...] = token.astype(f32)
    w_ref[...] = jnp.where(row < 4, w_first, w_second)
    for copy in coming[2:]:
        copy.wait()
    x_rows = jnp.dot(pick, x_ref[...], preferred_element_type=f32)
    g_rows = jnp.dot(pick, g_ref[...], preferred_element_type=f32)
    half = x_rows.shape[1] // 2
    quarter = half // 2
    at = lax.broadcasted_iota(jnp.int32, (8, half), 0)
    low = (at & 2) == 0
    unit = jnp.where(
        (at & 1) == 0,
        jnp.where(low, x_rows[:, :half], x_rows[:, half:]),
        jnp.where(low, g_rows[:, :half], g_rows[:, half:]),
    ).astype(bf16)
    for i in range(sent_ref.shape[0]):
        sent_ref[i] = unit
    at = lax.broadcasted_iota(jnp.int32, (8, quarter), 0) & 3
    cot = g_rows[:, :quarter]
    for q in range(1, 4):
        cot = jnp.where(at == q, g_rows[:, q * quarter : (q + 1) * quarter], cot)
    cot_ref[...] = cot


def weights_kernel(in_ref, out_ref, in_above_ref, out_above_ref, cot_hbm, w_all, cot_ref, sem):
    copy = pltpu.make_async_copy(cot_hbm, cot_ref, sem)
    copy.start()
    width, own = in_ref.shape[2], in_ref.shape[1]
    for kind in range(3):
        for i, (w_in, w_out) in enumerate(((in_ref, out_ref), (in_above_ref, out_above_ref))):
            at = kind * PAD + i * (PAD // 2)
            w_all[at + 48 : at + 64, :] = jnp.zeros((16, width), bf16)
            w_all[at : at + own, :] = w_in[kind] if kind < 2 else w_out[...]
    copy.wait()


def spread_kernel(column_ref, sent_ref, sems):
    copies = [
        pltpu.make_async_copy(column_ref, sent_ref.at[i], sems.at[i]) for i in range(sent_ref.shape[0])
    ]
    for copy in copies:
        copy.start()
    for copy in copies:
        copy.wait()


def expert_kernel(rows_hbm, w_all, part_hbm, rows_ref, prod, wide, part_ref, in_sems, out_sems):
    width = w_all.shape[1]
    half, quarter = width // 2, width // 4
    tall = rows_ref.shape[0]
    count = tall // 4
    pieces = in_sems.shape[0]
    height = tall // pieces
    coming = []
    for i in range(pieces):
        at = slice(i * height, (i + 1) * height)
        coming.append(pltpu.make_async_copy(rows_hbm.at[at], rows_ref.at[at], in_sems.at[i]))
        coming[i].start()
    nt = (((1,), (1,)), ((), ()))
    for i in range(pieces):
        at = slice(i * height, (i + 1) * height)
        coming[i].wait()
        for h in range(2):
            cols = slice(h * half, (h + 1) * half)
            out = lax.dot_general(
                rows_ref[at, :],
                w_all[:, cols],
                nt,
                preferred_element_type=f32,
            )
            for column in range(3):
                prod[h * 3 + column, at, :] = out[:, column * PAD : (column + 1) * PAD]

    def taken(kind, column):
        low = prod[column, pl.ds(kind, count, stride=4), :]
        return low + prod[3 + column, pl.ds(2 + kind, count, stride=4), :]

    gate, upper, d_hidden = taken(0, 0), taken(0, 1), taken(1, 2)
    sig = 1.0 / (1.0 + jnp.exp(-gate))
    hidden = (gate * sig * upper).astype(bf16)
    d_gate = (d_hidden * upper * sig * (1.0 + gate * (1.0 - sig))).astype(bf16)
    d_up = (d_hidden * gate * sig).astype(bf16)
    score = jnp.sum(hidden.astype(f32) * d_hidden, axis=1, keepdims=True)
    both = jnp.concatenate([d_gate, d_up], axis=1)
    blocks = quarter // 128
    going = []

    def send(at, blocks_there):
        for i in range(at, at + blocks_there):
            part_ref[:, i * 128 : (i + 1) * 128] = wide[i].astype(bf16)
        cols = slice(at * 128, (at + blocks_there) * 128)
        copy = pltpu.make_async_copy(part_ref.at[:, cols], part_hbm.at[:, cols], out_sems.at[len(going)])
        copy.start()
        going.append(copy)

    split_score(wide, blocks, jnp.broadcast_to(score, (count, 128)))
    send(blocks, 1)
    for at in range(0, blocks, 2):
        for q in range(4):
            cols = slice(q * quarter + at * 128, q * quarter + (at + 2) * 128)
            back = jnp.dot(both, w_all[: 2 * PAD, cols], preferred_element_type=f32)
            wide[at, pl.ds(q, count, stride=4), :] = back[:, :128]
            wide[at + 1, pl.ds(q, count, stride=4), :] = back[:, 128:]
        send(at, 2)
    for copy in going:
        copy.wait()


def split_score(wide, at, score):
    count = score.shape[0]
    for q in range(3):
        piece = score.astype(bf16).astype(f32)
        wide[at, pl.ds(q, count, stride=4), :] = piece
        score = score - piece
    wide[at, pl.ds(3, count, stride=4), :] = jnp.zeros_like(score)


def joined_score(wide, at, count):
    pieces = [wide[at, pl.ds(q, count, stride=4), :] for q in range(3)]
    return pieces[2] + pieces[1] + pieces[0]


def summed(got_ref):
    acc = got_ref[0].astype(f32)
    for i in range(1, got_ref.shape[0]):
        acc = acc + got_ref[i].astype(f32)
    return acc


def middle_kernel(got_ref, part_ref, wide):
    acc = summed(got_ref)
    at = acc.shape[1] - 128
    wide[0] = acc[:, at:]
    split_score(wide, 0, joined_score(wide, 0, acc.shape[0] // 4))
    part_ref[:, :at] = acc[:, :at].astype(bf16)
    part_ref[:, at:] = wide[0].astype(bf16)


def last_kernel(got_ref, cot_ref, w_ref, t_ref, held_ref, moved_ref, grad_ref, wide):
    acc = summed(got_ref)
    quarter = cot_ref.shape[1]
    wide[0] = acc[:, quarter:]
    back = acc[:, :quarter].astype(bf16).astype(f32)
    w = w_ref[:, :1]
    moved_ref[:, :quarter] = (cot_ref[...] + w * back).astype(bf16)
    moved_ref[:, quarter:] = t_ref[...].astype(bf16)
    score = joined_score(wide, 0, 2)
    grad_ref[...] = held_ref[0:2] * score[0:1] + held_ref[4:6] * score[1:2]


def place_kernel(cot_ref, moved_ref, out_ref, ready, sems):
    tokens, width = cot_ref.shape
    quarter = width // 4
    row = lax.broadcasted_iota(jnp.int32, (tokens, 128), 0).astype(f32)
    token = moved_ref[:, quarter:].astype(f32)
    at = [(row == token[4 * s : 4 * s + 1])[:, :1] for s in range(CAP)]
    copies = []
    for q in range(4):
        cols = slice(q * quarter, (q + 1) * quarter)
        value = cot_ref[:, cols].astype(f32)
        for s in range(CAP):
            value = jnp.where(at[s], moved_ref[4 * s + q : 4 * s + q + 1, :quarter].astype(f32), value)
        ready[:, cols] = value.astype(bf16)
        copies.append(pltpu.make_async_copy(ready.at[:, cols], out_ref.at[:, cols], sems.at[q]))
        copies[q].start()
    for copy in copies:
        copy.wait()


def call(kernel, outs, *operands, scratch=(), smem=(), near=(), far=(), out_space=pltpu.VMEM):
    def placed(i, v):
        if i in near or i in far:
            return pltpu.with_memory_space_constraint(v, pltpu.VMEM if i in near else pltpu.HBM)
        return v

    def space(i):
        return pltpu.SMEM if i in smem else pltpu.HBM if i in far else pltpu.VMEM

    return pl.pallas_call(
        kernel,
        out_shape=outs,
        in_specs=[pl.BlockSpec(memory_space=space(i)) for i in range(len(operands))],
        out_specs=[pl.BlockSpec(memory_space=out_space)] * len(outs),
        scratch_shapes=list(scratch),
        compiler_params=pltpu.CompilerParams(vmem_limit_bytes=24 << 20),
    )(*(placed(i, v) for i, v in enumerate(operands)))


def shape(dims, kind):
    return jax.ShapeDtypeStruct(dims, kind)


def on_device(layer_input, cotangent, route_weight, chosen, hot_expert, store_in, store_out):
    tokens, width = layer_input.shape[1:]
    half, quarter = width // 2, width // 4
    num_row = lax.axis_size("row")
    heights = num_row // PLANE
    peers = heights // 2
    along_z = [[a * 2 * PLANE + r for a in range(peers)] for r in range(2 * PLANE)]
    in_plane = [[z * PLANE + i for i in range(PLANE)] for z in range(heights)]
    sections = lax.axis_size("section")
    back_one = [(i, i - 1) for i in range(1, sections)]

    def exchange(value, groups):
        return lax.all_to_all(
            value, "row", split_axis=0, concat_axis=0, axis_index_groups=groups, tiled=True
        )

    def along(value, by):
        return lax.ppermute(value, "row", [(i, (i + by * PLANE) % num_row) for i in range(num_row)])

    w_in = jnp.swapaxes(store_in[0], 1, 2)
    w_out = store_out[0]
    in_above = along(w_in, -1)
    out_above = along(w_out, -1)
    cot_moved = lax.ppermute(cotangent[0], "section", back_one)

    unit, cot_rows, w_rows, t_rows, held = call(
        select_kernel,
        [
            pltpu.VMEM((peers, 8, half), bf16),
            pltpu.VMEM((8, quarter), f32),
            pltpu.VMEM((8, tokens), f32),
            pltpu.VMEM((8, tokens), f32),
            pltpu.VMEM((8, tokens), f32),
        ],
        chosen[0].T,
        hot_expert,
        route_weight[0].T,
        layer_input[0],
        cotangent[0],
        scratch=(
            pltpu.VMEM((TOP, tokens), jnp.int32),
            pltpu.VMEM((TOP, tokens), f32),
            pltpu.VMEM((tokens, width), bf16),
            pltpu.VMEM((tokens, width), bf16),
            pltpu.SemaphoreType.DMA((4,)),
        ),
        smem=(1,),
        far=(0, 2, 3, 4),
    )
    tall = peers * 8
    column = exchange(unit, along_z).reshape(tall, half)
    (sent,) = call(
        spread_kernel,
        [pltpu.HBM((PLANE, tall, half), bf16)],
        column,
        scratch=(pltpu.SemaphoreType.DMA((PLANE,)),),
        near=(0,),
        out_space=pltpu.HBM,
    )
    rows = exchange(sent, in_plane)
    w_all, cot_moved = call(
        weights_kernel,
        [pltpu.VMEM((3 * PAD, width), bf16), pltpu.VMEM((tokens, width), bf16)],
        w_in,
        w_out,
        in_above,
        out_above,
        cot_moved,
        scratch=(pltpu.SemaphoreType.DMA,),
        far=(4,),
    )
    wide = quarter + 128
    count = PLANE * tall
    (part,) = call(
        expert_kernel,
        [pltpu.HBM((count, wide), bf16)],
        rows.reshape(count, half),
        w_all,
        scratch=(
            pltpu.VMEM((count, half), bf16),
            pltpu.VMEM((6, count, PAD), f32),
            pltpu.VMEM((wide // 128, count, 128), f32),
            pltpu.VMEM((count, wide), bf16),
            pltpu.SemaphoreType.DMA((2,)),
            pltpu.SemaphoreType.DMA((5,)),
        ),
        near=(1,),
        far=(0,),
        out_space=pltpu.HBM,
    )
    got = exchange(part.reshape(PLANE, tall, wide), in_plane)
    (part,) = call(
        middle_kernel,
        [pltpu.VMEM((tall, wide), bf16)],
        got,
        scratch=(pltpu.VMEM((1, tall, 128), f32),),
        near=(0,),
    )
    got = exchange(part.reshape(peers, 8, wide), along_z)
    moved, grad = call(
        last_kernel,
        [pltpu.VMEM((8, wide), bf16), shape((2, tokens), f32)],
        got,
        cot_rows,
        w_rows,
        t_rows,
        held,
        scratch=(pltpu.VMEM((1, 8, 128), f32),),
        near=(0, 1, 2, 3, 4),
    )
    moved = lax.ppermute(moved, "section", back_one)
    (back_cot,) = call(
        place_kernel,
        [pltpu.HBM((tokens, width), bf16)],
        cot_moved,
        moved,
        scratch=(pltpu.VMEM((tokens, width), bf16), pltpu.SemaphoreType.DMA((4,))),
        near=(0, 1),
        out_space=pltpu.HBM,
    )
    return (back_cot[None], grad.T[None])


def solution(mesh):
    in_specs = (
        P("section", "row", None),
        P("section", "row", None),
        P("section", "row", None),
        P("section", "row", None),
        P("section"),
        P("section", None, None, "row"),
        P("section", "row", None),
    )
    out_specs = (P("section", "row", None), P("section", "row", None))

    return jax.shard_map(on_device, mesh=mesh, in_specs=in_specs, out_specs=out_specs, check_vma=False)
```

```python
import jax
import jax.numpy as jnp
from jax import lax
from jax.experimental import pallas as pl
from jax.experimental.pallas import tpu as pltpu
from jax.sharding import PartitionSpec as P


CAP = 2
TOP = 2
PLANE = 8
SENT_DOWN = 32
PAD = 128
NONE = 128

bf16 = jnp.bfloat16
f32 = jnp.float32


def slot_tokens(chosen, hot):
    hit = chosen == hot
    lane = lax.broadcasted_iota(jnp.int32, hit.shape, 1)
    at = jnp.where(hit, lane, NONE)
    first = jnp.min(jnp.min(at, axis=1, keepdims=True), axis=0, keepdims=True)
    later = jnp.where(at > first, at, NONE)
    second = jnp.min(jnp.min(later, axis=1, keepdims=True), axis=0, keepdims=True)
    return hit, lane, first, second


def total(values):
    return jnp.sum(jnp.sum(values, axis=1, keepdims=True), axis=0, keepdims=True)


def select_kernel(
    chosen_hbm, hot_ref, weight_hbm, x_hbm, g_hbm,
    sent_ref, cot_ref, w_ref, t_ref, held_ref,
    chosen_ref, weight_ref, x_ref, g_ref, sems,
):
    pairs = (
        (chosen_hbm, chosen_ref),
        (weight_hbm, weight_ref),
        (x_hbm, x_ref),
        (g_hbm, g_ref),
    )
    coming = [pltpu.make_async_copy(src, dst, sems.at[i]) for i, (src, dst) in enumerate(pairs)]
    for copy in coming:
        copy.start()
    for copy in coming[:2]:
        copy.wait()
    hit, lane, first, second = slot_tokens(chosen_ref[...], hot_ref[0])
    weights = weight_ref[...]
    in_first, in_second = hit & (lane == first), hit & (lane == second)
    held_ref[...] = jnp.zeros_like(held_ref)
    held_ref[0:2] = in_first.astype(f32)
    held_ref[4:6] = in_second.astype(f32)
    w_first = total(jnp.where(in_first, weights, 0.0))
    w_second = total(jnp.where(in_second, weights, 0.0))
    tokens = x_ref.shape[0]
    row = lax.broadcasted_iota(jnp.int32, (8, tokens), 0)
    col = lax.broadcasted_iota(jnp.int32, (8, tokens), 1)
    token = jnp.where(row < 4, first, second)
    pick = (col == token).astype(f32).astype(bf16)
    t_ref[...] = token.astype(f32)
    w_ref[...] = jnp.where(row < 4, w_first, w_second)
    for copy in coming[2:]:
        copy.wait()
    x_rows = jnp.dot(pick, x_ref[...], preferred_element_type=f32)
    g_rows = jnp.dot(pick, g_ref[...], preferred_element_type=f32)
    half = x_rows.shape[1] // 2
    quarter = half // 2
    at = lax.broadcasted_iota(jnp.int32, (8, half), 0)
    low = (at & 2) == 0
    unit = jnp.where(
        (at & 1) == 0,
        jnp.where(low, x_rows[:, :half], x_rows[:, half:]),
        jnp.where(low, g_rows[:, :half], g_rows[:, half:]),
    ).astype(bf16)
    for i in range(sent_ref.shape[0]):
        sent_ref[i] = unit
    at = lax.broadcasted_iota(jnp.int32, (8, quarter), 0) & 3
    cot = g_rows[:, :quarter]
    for q in range(1, 4):
        cot = jnp.where(at == q, g_rows[:, q * quarter : (q + 1) * quarter], cot)
    cot_ref[...] = cot


def weights_kernel(in_ref, out_ref, below_ref, above_ref, w_all):
    width, own = in_ref.shape[2], in_ref.shape[1]
    n_above, n_below = above_ref.shape[1], below_ref.shape[1]
    for kind in range(3):
        at = kind * PAD
        w_all[at + 48 : at + 64, :] = jnp.zeros((16, width), bf16)
        w_all[at + 112 : at + 128, :] = jnp.zeros((16, width), bf16)
        w_all[at : at + n_above, :] = above_ref[kind]
        w_all[at + n_above : at + n_above + n_below, :] = below_ref[kind]
        w_all[at + 64 : at + 64 + own, :] = in_ref[kind] if kind < 2 else out_ref[...]


def spread_kernel(column_ref, sent_ref, sems):
    copies = [
        pltpu.make_async_copy(column_ref, sent_ref.at[i], sems.at[i]) for i in range(sent_ref.shape[0])
    ]
    for copy in copies:
        copy.start()
    for copy in copies:
        copy.wait()


def expert_kernel(rows_hbm, w_all, _, part_ref, rows_ref, prod, wide, in_sems):
    width = w_all.shape[1]
    half, quarter = width // 2, width // 4
    count = rows_ref.shape[0] // 4
    pieces = in_sems.shape[0]
    height = rows_ref.shape[0] // pieces
    coming = []
    for i in range(pieces):
        at = slice(i * height, (i + 1) * height)
        coming.append(pltpu.make_async_copy(rows_hbm.at[at], rows_ref.at[at], in_sems.at[i]))
        coming[i].start()
    nt = (((1,), (1,)), ((), ()))
    for i in range(pieces):
        at = slice(i * height, (i + 1) * height)
        coming[i].wait()
        for h in range(2):
            cols = slice(h * half, (h + 1) * half)
            out = lax.dot_general(
                rows_ref[at, :],
                w_all[:, cols],
                nt,
                preferred_element_type=f32,
            )
            for column in range(3):
                prod[h * 3 + column, at, :] = out[:, column * PAD : (column + 1) * PAD]

    def taken(kind, column):
        low = prod[column, pl.ds(kind, count, stride=4), :]
        return low + prod[3 + column, pl.ds(2 + kind, count, stride=4), :]

    gate, upper, d_hidden = taken(0, 0), taken(0, 1), taken(1, 2)
    sig = 1.0 / (1.0 + jnp.exp(-gate))
    hidden = (gate * sig * upper).astype(bf16)
    d_gate = (d_hidden * upper * sig * (1.0 + gate * (1.0 - sig))).astype(bf16)
    d_up = (d_hidden * gate * sig).astype(bf16)
    score = jnp.sum(hidden.astype(f32) * d_hidden, axis=1, keepdims=True)
    both = jnp.concatenate([d_gate, d_up], axis=1)
    peers, tall = part_ref.shape[0], rows_ref.shape[0] // part_ref.shape[0]
    blocks = quarter // 128
    part_ref[:, blocks * tall :, :] = score_pieces(score).reshape(peers, tall // 4, 128).astype(bf16)
    for at in range(0, blocks, 2):
        for q in range(4):
            cols = slice(q * quarter + at * 128, q * quarter + (at + 2) * 128)
            back = jnp.dot(both, w_all[: 2 * PAD, cols], preferred_element_type=f32)
            wide[at, pl.ds(q, count, stride=4), :] = back[:, :128]
            wide[at + 1, pl.ds(q, count, stride=4), :] = back[:, 128:]
        for i in (at, at + 1):
            part_ref[:, i * tall : (i + 1) * tall, :] = wide[i].reshape(peers, tall, 128).astype(bf16)


def score_pieces(score):
    lane = lax.broadcasted_iota(jnp.int32, (score.shape[0], 128), 1)
    rest = jnp.broadcast_to(score, lane.shape)
    out = jnp.zeros_like(rest)
    for i in range(3):
        piece = rest.astype(bf16).astype(f32)
        out = jnp.where(lane == i, piece, out)
        rest = rest - piece
    return out


def summed(got_ref):
    acc = got_ref[0].astype(f32)
    for i in range(1, got_ref.shape[0]):
        acc = acc + got_ref[i].astype(f32)
    return acc


def middle_kernel(got_ref, cot_hbm, part_ref, cot_ref, tile, scores, sem):
    copy = pltpu.make_async_copy(cot_hbm, cot_ref, sem)
    copy.start()
    peers = part_ref.shape[0]
    tall = peers * 8
    acc = summed(got_ref)
    blocks = (acc.shape[0] - tall // 4) // tall
    for i in range(blocks):
        rows = acc[i * tall : (i + 1) * tall].reshape(peers, 8, 128)
        part_ref[:, i * 8 : (i + 1) * 8, :] = rows.astype(bf16)
    scores[...] = score_pieces(jnp.sum(acc[blocks * tall :], axis=1, keepdims=True))
    tile[...] = jnp.zeros_like(tile)
    for a in range(peers):
        tile[a, 0:CAP] = scores[CAP * a : CAP * (a + 1)]
    part_ref[:, blocks * 8 :, :] = tile[...].astype(bf16)
    copy.wait()


def last_kernel(got_ref, cot_ref, w_ref, t_ref, held_ref, moved_ref, grad_ref):
    acc = summed(got_ref)
    quarter = cot_ref.shape[1]
    w = w_ref[...]
    for i in range(quarter // 128):
        cols = slice(i * 128, (i + 1) * 128)
        back = acc[i * 8 : (i + 1) * 8].astype(bf16).astype(f32)
        moved_ref[:, cols] = (cot_ref[:, cols] + w * back).astype(bf16)
    moved_ref[:, quarter:] = t_ref[...].astype(bf16)
    score = jnp.sum(acc[quarter // 16 :], axis=1, keepdims=True)
    grad_ref[...] = held_ref[0:2] * score[0:1] + held_ref[4:6] * score[1:2]


def place_kernel(cot_ref, moved_ref, out_ref, ready, sems):
    tokens, width = cot_ref.shape
    quarter = width // 4
    row = lax.broadcasted_iota(jnp.int32, (tokens, 128), 0).astype(f32)
    token = moved_ref[:, quarter:].astype(f32)
    at = [(row == token[4 * s : 4 * s + 1])[:, :1] for s in range(CAP)]
    copies = []
    for q in range(4):
        cols = slice(q * quarter, (q + 1) * quarter)
        value = cot_ref[:, cols].astype(f32)
        for s in range(CAP):
            value = jnp.where(at[s], moved_ref[4 * s + q : 4 * s + q + 1, :quarter].astype(f32), value)
        ready[:, cols] = value.astype(bf16)
        copies.append(pltpu.make_async_copy(ready.at[:, cols], out_ref.at[:, cols], sems.at[q]))
        copies[q].start()
    for copy in copies:
        copy.wait()


def call(kernel, outs, *operands, scratch=(), smem=(), near=(), far=(), out_space=pltpu.VMEM):
    def placed(i, v):
        if i in near or i in far:
            return pltpu.with_memory_space_constraint(v, pltpu.VMEM if i in near else pltpu.HBM)
        return v

    def space(i):
        return pltpu.SMEM if i in smem else pltpu.HBM if i in far else pltpu.VMEM

    return pl.pallas_call(
        kernel,
        out_shape=outs,
        in_specs=[pl.BlockSpec(memory_space=space(i)) for i in range(len(operands))],
        out_specs=[pl.BlockSpec(memory_space=out_space)] * len(outs),
        scratch_shapes=list(scratch),
        compiler_params=pltpu.CompilerParams(vmem_limit_bytes=24 << 20),
    )(*(placed(i, v) for i, v in enumerate(operands)))


def shape(dims, kind):
    return jax.ShapeDtypeStruct(dims, kind)


def on_device(layer_input, cotangent, route_weight, chosen, hot_expert, store_in, store_out):
    tokens, width = layer_input.shape[1:]
    half, quarter = width // 2, width // 4
    num_row = lax.axis_size("row")
    heights = num_row // PLANE
    peers = heights // 2
    along_z = [[a * 2 * PLANE + r for a in range(peers)] for r in range(2 * PLANE)]
    in_plane = [[z * PLANE + i for i in range(PLANE)] for z in range(heights)]
    sections = lax.axis_size("section")
    back_one = [(i, i - 1) for i in range(1, sections)]

    def exchange(value, groups):
        return lax.all_to_all(
            value, "row", split_axis=0, concat_axis=0, axis_index_groups=groups, tiled=True
        )

    def along(value, by):
        return lax.ppermute(value, "row", [(i, (i + by * PLANE) % num_row) for i in range(num_row)])

    w_in = jnp.swapaxes(store_in[0], 1, 2)
    w_out = store_out[0]
    w_both = jnp.concatenate([w_in, w_out[None]], axis=0)
    from_above = along(w_both[:, :SENT_DOWN], -1)
    from_below = along(w_both[:, SENT_DOWN:], 1)
    cot_moved = lax.ppermute(cotangent[0], "section", back_one)

    unit, cot_rows, w_rows, t_rows, held = call(
        select_kernel,
        [
            pltpu.VMEM((peers, 8, half), bf16),
            pltpu.VMEM((8, quarter), f32),
            pltpu.VMEM((8, tokens), f32),
            pltpu.VMEM((8, tokens), f32),
            pltpu.VMEM((8, tokens), f32),
        ],
        chosen[0].T,
        hot_expert,
        route_weight[0].T,
        layer_input[0],
        cotangent[0],
        scratch=(
            pltpu.VMEM((TOP, tokens), jnp.int32),
            pltpu.VMEM((TOP, tokens), f32),
            pltpu.VMEM((tokens, width), bf16),
            pltpu.VMEM((tokens, width), bf16),
            pltpu.SemaphoreType.DMA((4,)),
        ),
        smem=(1,),
        far=(0, 2, 3, 4),
    )
    tall = peers * 8
    column = exchange(unit, along_z).reshape(tall, half)
    (sent,) = call(
        spread_kernel,
        [pltpu.HBM((PLANE, tall, half), bf16)],
        column,
        scratch=(pltpu.SemaphoreType.DMA((PLANE,)),),
        near=(0,),
        out_space=pltpu.HBM,
    )
    rows = exchange(sent, in_plane)
    (w_all,) = call(
        weights_kernel,
        [pltpu.VMEM((3 * PAD, width), bf16)],
        w_in,
        w_out,
        from_below,
        from_above,
        near=(0, 1, 2, 3),
    )
    count = PLANE * tall
    (part,) = call(
        expert_kernel,
        [pltpu.VMEM((PLANE, quarter // 128 * tall + tall // 4, 128), bf16)],
        rows.reshape(count, half),
        w_all,
        cot_moved,
        scratch=(
            pltpu.VMEM((count, half), bf16),
            pltpu.VMEM((6, count, PAD), f32),
            pltpu.VMEM((quarter // 128, count, 128), f32),
            pltpu.SemaphoreType.DMA((4,)),
        ),
        near=(1,),
        far=(0, 2),
    )
    got = exchange(part, in_plane)
    part, cot_moved = call(
        middle_kernel,
        [pltpu.VMEM((peers, quarter // 16 + 8, 128), bf16), pltpu.VMEM((tokens, width), bf16)],
        got,
        cot_moved,
        scratch=(
            pltpu.VMEM((peers, 8, 128), f32),
            pltpu.VMEM((peers * CAP, 128), f32),
            pltpu.SemaphoreType.DMA,
        ),
        near=(0,),
        far=(1,),
    )
    got = exchange(part, along_z)
    moved, grad = call(
        last_kernel,
        [pltpu.VMEM((8, quarter + 128), bf16), shape((TOP, tokens), f32)],
        got,
        cot_rows,
        w_rows,
        t_rows,
        held,
        near=(0, 1, 2, 3, 4),
    )
    moved = lax.ppermute(moved, "section", back_one)
    (back_cot,) = call(
        place_kernel,
        [pltpu.HBM((tokens, width), bf16)],
        cot_moved,
        moved,
        scratch=(pltpu.VMEM((tokens, width), bf16), pltpu.SemaphoreType.DMA((4,))),
        near=(0, 1),
        out_space=pltpu.HBM,
    )
    return (back_cot[None], grad.T[None])


def solution(mesh):
    in_specs = (
        P("section", "row", None),
        P("section", "row", None),
        P("section", "row", None),
        P("section", "row", None),
        P("section"),
        P("section", None, None, "row"),
        P("section", "row", None),
    )
    out_specs = (P("section", "row", None), P("section", "row", None))

    return jax.shard_map(on_device, mesh=mesh, in_specs=in_specs, out_specs=out_specs, check_vma=False)
```

```python
import jax
import jax.numpy as jnp
from jax import lax
from jax.experimental import pallas as pl
from jax.experimental.pallas import tpu as pltpu
from jax.sharding import PartitionSpec as P


CAP = 2
TOP = 2
PLANE = 8
SENT_DOWN = 32
PAD = 128
NONE = 128

bf16 = jnp.bfloat16
f32 = jnp.float32


def slot_tokens(chosen, hot):
    hit = chosen == hot
    lane = lax.broadcasted_iota(jnp.int32, hit.shape, 1)
    at = jnp.where(hit, lane, NONE)
    first = jnp.min(jnp.min(at, axis=1, keepdims=True), axis=0, keepdims=True)
    later = jnp.where(at > first, at, NONE)
    second = jnp.min(jnp.min(later, axis=1, keepdims=True), axis=0, keepdims=True)
    return hit, lane, first, second


def total(values):
    return jnp.sum(jnp.sum(values, axis=1, keepdims=True), axis=0, keepdims=True)


def select_kernel(
    chosen_hbm, hot_ref, weight_hbm, x_hbm, g_hbm,
    sent_ref, cot_ref, w_ref, t_ref, held_ref,
    chosen_ref, weight_ref, x_ref, g_ref, sems,
):
    pairs = (
        (chosen_hbm, chosen_ref),
        (weight_hbm, weight_ref),
        (x_hbm, x_ref),
        (g_hbm, g_ref),
    )
    coming = [pltpu.make_async_copy(src, dst, sems.at[i]) for i, (src, dst) in enumerate(pairs)]
    for copy in coming:
        copy.start()
    for copy in coming[:2]:
        copy.wait()
    hit, lane, first, second = slot_tokens(chosen_ref[...], hot_ref[0])
    weights = weight_ref[...]
    in_first, in_second = hit & (lane == first), hit & (lane == second)
    held_ref[...] = jnp.zeros_like(held_ref)
    held_ref[0:2] = in_first.astype(f32)
    held_ref[4:6] = in_second.astype(f32)
    w_first = total(jnp.where(in_first, weights, 0.0))
    w_second = total(jnp.where(in_second, weights, 0.0))
    tokens = x_ref.shape[0]
    row = lax.broadcasted_iota(jnp.int32, (8, tokens), 0)
    col = lax.broadcasted_iota(jnp.int32, (8, tokens), 1)
    token = jnp.where(row < 4, first, second)
    pick = (col == token).astype(f32).astype(bf16)
    t_ref[...] = token.astype(f32)
    w_ref[...] = jnp.where(row < 4, w_first, w_second)
    for copy in coming[2:]:
        copy.wait()
    x_rows = jnp.dot(pick, x_ref[...], preferred_element_type=f32)
    g_rows = jnp.dot(pick, g_ref[...], preferred_element_type=f32)
    half = x_rows.shape[1] // 2
    quarter = half // 2
    at = lax.broadcasted_iota(jnp.int32, (8, half), 0)
    low = (at & 2) == 0
    unit = jnp.where(
        (at & 1) == 0,
        jnp.where(low, x_rows[:, :half], x_rows[:, half:]),
        jnp.where(low, g_rows[:, :half], g_rows[:, half:]),
    ).astype(bf16)
    for i in range(sent_ref.shape[0]):
        sent_ref[i] = unit
    at = lax.broadcasted_iota(jnp.int32, (8, quarter), 0) & 3
    cot = g_rows[:, :quarter]
    for q in range(1, 4):
        cot = jnp.where(at == q, g_rows[:, q * quarter : (q + 1) * quarter], cot)
    cot_ref[...] = cot


def weights_kernel(in_ref, out_ref, below_ref, above_ref, w_all):
    width, own = in_ref.shape[2], in_ref.shape[1]
    n_above, n_below = above_ref.shape[1], below_ref.shape[1]
    for kind in range(3):
        at = kind * PAD
        w_all[at + 48 : at + 64, :] = jnp.zeros((16, width), bf16)
        w_all[at + 112 : at + 128, :] = jnp.zeros((16, width), bf16)
        w_all[at : at + n_above, :] = above_ref[kind]
        w_all[at + n_above : at + n_above + n_below, :] = below_ref[kind]
        w_all[at + 64 : at + 64 + own, :] = in_ref[kind] if kind < 2 else out_ref[...]


def spread_kernel(column_ref, sent_ref, sems):
    copies = [
        pltpu.make_async_copy(column_ref, sent_ref.at[i], sems.at[i]) for i in range(sent_ref.shape[0])
    ]
    for copy in copies:
        copy.start()
    for copy in copies:
        copy.wait()


def expert_kernel(rows_hbm, w_all, part_ref, rows_ref, prod, wide, sem):
    width = w_all.shape[1]
    half, quarter = width // 2, width // 4
    count = rows_ref.shape[0] // 4
    coming = pltpu.make_async_copy(rows_hbm, rows_ref, sem)
    coming.start()
    coming.wait()
    nt = (((1,), (1,)), ((), ()))
    for h in range(2):
        cols = slice(h * half, (h + 1) * half)
        out = lax.dot_general(rows_ref[...], w_all[:, cols], nt, preferred_element_type=f32)
        for column in range(3):
            prod[h * 3 + column] = out[:, column * PAD : (column + 1) * PAD]

    def taken(kind, column):
        low = prod[column, pl.ds(kind, count, stride=4), :]
        return low + prod[3 + column, pl.ds(2 + kind, count, stride=4), :]

    gate, upper, d_hidden = taken(0, 0), taken(0, 1), taken(1, 2)
    sig = 1.0 / (1.0 + jnp.exp(-gate))
    hidden = (gate * sig * upper).astype(bf16)
    d_gate = (d_hidden * upper * sig * (1.0 + gate * (1.0 - sig))).astype(bf16)
    d_up = (d_hidden * gate * sig).astype(bf16)
    score = jnp.sum(hidden.astype(f32) * d_hidden, axis=1, keepdims=True)
    both = jnp.concatenate([d_gate, d_up], axis=1)
    peers, tall = part_ref.shape[0], rows_ref.shape[0] // part_ref.shape[0]
    blocks = quarter // 128
    part_ref[:, blocks * tall :, :] = score_pieces(score).reshape(peers, tall // 4, 128).astype(bf16)
    for at in range(0, blocks, 2):
        for q in range(4):
            cols = slice(q * quarter + at * 128, q * quarter + (at + 2) * 128)
            back = jnp.dot(both, w_all[: 2 * PAD, cols], preferred_element_type=f32)
            wide[at, pl.ds(q, count, stride=4), :] = back[:, :128]
            wide[at + 1, pl.ds(q, count, stride=4), :] = back[:, 128:]
        for i in (at, at + 1):
            part_ref[:, i * tall : (i + 1) * tall, :] = wide[i].reshape(peers, tall, 128).astype(bf16)


def score_pieces(score):
    lane = lax.broadcasted_iota(jnp.int32, (score.shape[0], 128), 1)
    rest = jnp.broadcast_to(score, lane.shape)
    out = jnp.zeros_like(rest)
    for i in range(3):
        piece = rest.astype(bf16).astype(f32)
        out = jnp.where(lane == i, piece, out)
        rest = rest - piece
    return out


def summed(got_ref):
    acc = got_ref[0].astype(f32)
    for i in range(1, got_ref.shape[0]):
        acc = acc + got_ref[i].astype(f32)
    return acc


def middle_kernel(got_ref, part_hbm, part_ref, tile, scores, sem):
    peers = part_ref.shape[0]
    tall = peers * 8
    acc = summed(got_ref)
    blocks = (acc.shape[0] - tall // 4) // tall
    for i in range(blocks):
        rows = acc[i * tall : (i + 1) * tall].reshape(peers, 8, 128)
        part_ref[:, i * 8 : (i + 1) * 8, :] = rows.astype(bf16)
    scores[...] = score_pieces(jnp.sum(acc[blocks * tall :], axis=1, keepdims=True))
    tile[...] = jnp.zeros_like(tile)
    for a in range(peers):
        tile[a, 0:CAP] = scores[CAP * a : CAP * (a + 1)]
    part_ref[:, blocks * 8 :, :] = tile[...].astype(bf16)
    copy = pltpu.make_async_copy(part_ref, part_hbm, sem)
    copy.start()
    copy.wait()


def last_kernel(got_ref, cot_ref, w_ref, t_ref, held_ref, moved_ref, grad_ref):
    acc = summed(got_ref)
    quarter = cot_ref.shape[1]
    w = w_ref[...]
    for i in range(quarter // 128):
        cols = slice(i * 128, (i + 1) * 128)
        back = acc[i * 8 : (i + 1) * 8].astype(bf16).astype(f32)
        moved_ref[:, cols] = (cot_ref[:, cols] + w * back).astype(bf16)
    moved_ref[:, quarter:] = t_ref[...].astype(bf16)
    score = jnp.sum(acc[quarter // 16 :], axis=1, keepdims=True)
    grad_ref[...] = held_ref[0:2] * score[0:1] + held_ref[4:6] * score[1:2]


def place_kernel(cot_ref, moved_ref, out_ref, ready, sems):
    tokens, width = cot_ref.shape
    quarter = width // 4
    row = lax.broadcasted_iota(jnp.int32, (tokens, 128), 0).astype(f32)
    token = moved_ref[:, quarter:].astype(f32)
    at = [(row == token[4 * s : 4 * s + 1])[:, :1] for s in range(CAP)]
    copies = []
    for q in range(4):
        cols = slice(q * quarter, (q + 1) * quarter)
        value = cot_ref[:, cols].astype(f32)
        for s in range(CAP):
            value = jnp.where(at[s], moved_ref[4 * s + q : 4 * s + q + 1, :quarter].astype(f32), value)
        ready[:, cols] = value.astype(bf16)
        copies.append(pltpu.make_async_copy(ready.at[:, cols], out_ref.at[:, cols], sems.at[q]))
        copies[q].start()
    for copy in copies:
        copy.wait()


def call(kernel, outs, *operands, scratch=(), smem=(), near=(), far=(), out_space=pltpu.VMEM):
    def placed(i, v):
        if i in near or i in far:
            return pltpu.with_memory_space_constraint(v, pltpu.VMEM if i in near else pltpu.HBM)
        return v

    def space(i):
        return pltpu.SMEM if i in smem else pltpu.HBM if i in far else pltpu.VMEM

    return pl.pallas_call(
        kernel,
        out_shape=outs,
        in_specs=[pl.BlockSpec(memory_space=space(i)) for i in range(len(operands))],
        out_specs=[pl.BlockSpec(memory_space=out_space)] * len(outs),
        scratch_shapes=list(scratch),
        compiler_params=pltpu.CompilerParams(vmem_limit_bytes=24 << 20),
    )(*(placed(i, v) for i, v in enumerate(operands)))


def shape(dims, kind):
    return jax.ShapeDtypeStruct(dims, kind)


def on_device(layer_input, cotangent, route_weight, chosen, hot_expert, store_in, store_out):
    tokens, width = layer_input.shape[1:]
    half, quarter = width // 2, width // 4
    num_row = lax.axis_size("row")
    heights = num_row // PLANE
    peers = heights // 2
    along_z = [[a * 2 * PLANE + r for a in range(peers)] for r in range(2 * PLANE)]
    in_plane = [[z * PLANE + i for i in range(PLANE)] for z in range(heights)]
    sections = lax.axis_size("section")
    back_one = [(i, i - 1) for i in range(1, sections)]

    def exchange(value, groups):
        return lax.all_to_all(
            value, "row", split_axis=0, concat_axis=0, axis_index_groups=groups, tiled=True
        )

    def along(value, by):
        return lax.ppermute(value, "row", [(i, (i + by * PLANE) % num_row) for i in range(num_row)])

    w_in = jnp.swapaxes(store_in[0], 1, 2)
    w_out = store_out[0]
    w_both = jnp.concatenate([w_in, w_out[None]], axis=0)
    from_above = along(w_both[:, :SENT_DOWN], -1)
    from_below = along(w_both[:, SENT_DOWN:], 1)
    cot_moved = lax.ppermute(cotangent[0], "section", back_one)

    unit, cot_rows, w_rows, t_rows, held = call(
        select_kernel,
        [
            pltpu.VMEM((peers, 8, half), bf16),
            pltpu.VMEM((8, quarter), f32),
            pltpu.VMEM((8, tokens), f32),
            pltpu.VMEM((8, tokens), f32),
            pltpu.VMEM((8, tokens), f32),
        ],
        chosen[0].T,
        hot_expert,
        route_weight[0].T,
        layer_input[0],
        cotangent[0],
        scratch=(
            pltpu.VMEM((TOP, tokens), jnp.int32),
            pltpu.VMEM((TOP, tokens), f32),
            pltpu.VMEM((tokens, width), bf16),
            pltpu.VMEM((tokens, width), bf16),
            pltpu.SemaphoreType.DMA((4,)),
        ),
        smem=(1,),
        far=(0, 2, 3, 4),
    )
    tall = peers * 8
    column = exchange(unit, along_z).reshape(tall, half)
    (sent,) = call(
        spread_kernel,
        [pltpu.HBM((PLANE, tall, half), bf16)],
        column,
        scratch=(pltpu.SemaphoreType.DMA((PLANE,)),),
        near=(0,),
        out_space=pltpu.HBM,
    )
    rows = exchange(sent, in_plane)
    (w_all,) = call(
        weights_kernel,
        [pltpu.VMEM((3 * PAD, width), bf16)],
        w_in,
        w_out,
        from_below,
        from_above,
        near=(0, 1, 2, 3),
    )
    count = PLANE * tall
    (part,) = call(
        expert_kernel,
        [pltpu.VMEM((PLANE, quarter // 128 * tall + tall // 4, 128), bf16)],
        rows.reshape(count, half),
        w_all,
        scratch=(
            pltpu.VMEM((count, half), bf16),
            pltpu.VMEM((6, count, PAD), f32),
            pltpu.VMEM((quarter // 128, count, 128), f32),
            pltpu.SemaphoreType.DMA,
        ),
        near=(1,),
        far=(0,),
    )
    got = exchange(part, in_plane)
    part_shape = (peers, quarter // 16 + 8, 128)
    (part,) = call(
        middle_kernel,
        [pltpu.HBM(part_shape, bf16)],
        got,
        scratch=(
            pltpu.VMEM(part_shape, bf16),
            pltpu.VMEM((peers, 8, 128), f32),
            pltpu.VMEM((peers * CAP, 128), f32),
            pltpu.SemaphoreType.DMA,
        ),
        near=(0,),
        out_space=pltpu.HBM,
    )
    got = exchange(part, along_z)
    moved, grad = call(
        last_kernel,
        [pltpu.VMEM((8, quarter + 128), bf16), shape((TOP, tokens), f32)],
        got,
        cot_rows,
        w_rows,
        t_rows,
        held,
        near=(0, 1, 2, 3, 4),
    )
    moved = lax.ppermute(moved, "section", back_one)
    (back_cot,) = call(
        place_kernel,
        [pltpu.HBM((tokens, width), bf16)],
        cot_moved,
        moved,
        scratch=(pltpu.VMEM((tokens, width), bf16), pltpu.SemaphoreType.DMA((4,))),
        near=(0, 1),
        out_space=pltpu.HBM,
    )
    return (back_cot[None], grad.T[None])


def solution(mesh):
    in_specs = (
        P("section", "row", None),
        P("section", "row", None),
        P("section", "row", None),
        P("section", "row", None),
        P("section"),
        P("section", None, None, "row"),
        P("section", "row", None),
    )
    out_specs = (P("section", "row", None), P("section", "row", None))

    return jax.shard_map(on_device, mesh=mesh, in_specs=in_specs, out_specs=out_specs, check_vma=False)
```

```python
import jax
import jax.numpy as jnp
from jax import lax
from jax.experimental import pallas as pl
from jax.experimental.pallas import tpu as pltpu
from jax.sharding import PartitionSpec as P


CAP = 2
TOP = 2
TURNS = 2200
PLANE = 8
SENT_DOWN = 32
PAD = 128
NONE = 128

bf16 = jnp.bfloat16
f32 = jnp.float32


def slot_tokens(chosen, hot):
    hit = chosen == hot
    lane = lax.broadcasted_iota(jnp.int32, hit.shape, 1)
    at = jnp.where(hit, lane, NONE)
    first = jnp.min(jnp.min(at, axis=1, keepdims=True), axis=0, keepdims=True)
    later = jnp.where(at > first, at, NONE)
    second = jnp.min(jnp.min(later, axis=1, keepdims=True), axis=0, keepdims=True)
    return hit, lane, first, second


def total(values):
    return jnp.sum(jnp.sum(values, axis=1, keepdims=True), axis=0, keepdims=True)


def select_kernel(
    chosen_hbm, hot_ref, weight_hbm, x_hbm, g_hbm, turns_ref,
    sent_ref, cot_ref, w_ref, t_ref, held_ref,
    chosen_ref, weight_ref, x_ref, g_ref, spun_ref, sems,
):
    pairs = (
        (chosen_hbm, chosen_ref),
        (weight_hbm, weight_ref),
        (x_hbm, x_ref),
        (g_hbm, g_ref),
    )
    coming = [pltpu.make_async_copy(src, dst, sems.at[i]) for i, (src, dst) in enumerate(pairs)]
    for copy in coming:
        copy.start()
    for copy in coming[:2]:
        copy.wait()
    hit, lane, first, second = slot_tokens(chosen_ref[...], hot_ref[0])
    weights = weight_ref[...]
    in_first, in_second = hit & (lane == first), hit & (lane == second)
    held_ref[...] = jnp.zeros_like(held_ref)
    held_ref[0:2] = in_first.astype(f32)
    held_ref[4:6] = in_second.astype(f32)
    w_first = total(jnp.where(in_first, weights, 0.0))
    w_second = total(jnp.where(in_second, weights, 0.0))
    tokens = x_ref.shape[0]
    row = lax.broadcasted_iota(jnp.int32, (8, tokens), 0)
    col = lax.broadcasted_iota(jnp.int32, (8, tokens), 1)
    token = jnp.where(row < 4, first, second)
    pick = (col == token).astype(f32).astype(bf16)
    t_ref[...] = token.astype(f32)
    w_ref[...] = jnp.where(row < 4, w_first, w_second)
    for copy in coming[2:]:
        copy.wait()
    x_rows = jnp.dot(pick, x_ref[...], preferred_element_type=f32)
    g_rows = jnp.dot(pick, g_ref[...], preferred_element_type=f32)
    half = x_rows.shape[1] // 2
    quarter = half // 2
    at = lax.broadcasted_iota(jnp.int32, (8, half), 0)
    low = (at & 2) == 0
    unit = jnp.where(
        (at & 1) == 0,
        jnp.where(low, x_rows[:, :half], x_rows[:, half:]),
        jnp.where(low, g_rows[:, :half], g_rows[:, half:]),
    ).astype(bf16)
    for i in range(sent_ref.shape[0]):
        sent_ref[i] = unit

    def turn(i, carry):
        spun_ref[...] = spun_ref[...] + 1.0
        return carry

    spun_ref[...] = jnp.zeros_like(spun_ref)
    lax.fori_loop(0, turns_ref[0], turn, 0)
    at = lax.broadcasted_iota(jnp.int32, (8, quarter), 0) & 3
    cot = g_rows[:, :quarter]
    for q in range(1, 4):
        cot = jnp.where(at == q, g_rows[:, q * quarter : (q + 1) * quarter], cot)
    cot_ref[...] = cot


def weights_kernel(in_ref, out_ref, below_ref, above_ref, w_all):
    width, own = in_ref.shape[2], in_ref.shape[1]
    n_above, n_below = above_ref.shape[1], below_ref.shape[1]
    for kind in range(3):
        at = kind * PAD
        w_all[at + 48 : at + 64, :] = jnp.zeros((16, width), bf16)
        w_all[at + 112 : at + 128, :] = jnp.zeros((16, width), bf16)
        w_all[at : at + n_above, :] = above_ref[kind]
        w_all[at + n_above : at + n_above + n_below, :] = below_ref[kind]
        w_all[at + 64 : at + 64 + own, :] = in_ref[kind] if kind < 2 else out_ref[...]


def spread_kernel(column_ref, sent_ref, sems):
    copies = [
        pltpu.make_async_copy(column_ref, sent_ref.at[i], sems.at[i]) for i in range(sent_ref.shape[0])
    ]
    for copy in copies:
        copy.start()
    for copy in copies:
        copy.wait()


def expert_kernel(rows_hbm, w_all, part_ref, rows_ref, prod, wide, sem):
    width = w_all.shape[1]
    half, quarter = width // 2, width // 4
    count = rows_ref.shape[0] // 4
    coming = pltpu.make_async_copy(rows_hbm, rows_ref, sem)
    coming.start()
    coming.wait()
    nt = (((1,), (1,)), ((), ()))
    for h in range(2):
        cols = slice(h * half, (h + 1) * half)
        out = lax.dot_general(rows_ref[...], w_all[:, cols], nt, preferred_element_type=f32)
        for column in range(3):
            prod[h * 3 + column] = out[:, column * PAD : (column + 1) * PAD]

    def taken(kind, column):
        low = prod[column, pl.ds(kind, count, stride=4), :]
        return low + prod[3 + column, pl.ds(2 + kind, count, stride=4), :]

    gate, upper, d_hidden = taken(0, 0), taken(0, 1), taken(1, 2)
    sig = 1.0 / (1.0 + jnp.exp(-gate))
    hidden = (gate * sig * upper).astype(bf16)
    d_gate = (d_hidden * upper * sig * (1.0 + gate * (1.0 - sig))).astype(bf16)
    d_up = (d_hidden * gate * sig).astype(bf16)
    score = jnp.sum(hidden.astype(f32) * d_hidden, axis=1, keepdims=True)
    both = jnp.concatenate([d_gate, d_up], axis=1)
    peers, tall = part_ref.shape[0], rows_ref.shape[0] // part_ref.shape[0]
    blocks = quarter // 128
    part_ref[:, blocks * tall :, :] = score_pieces(score).reshape(peers, tall // 4, 128).astype(bf16)
    for at in range(0, blocks, 2):
        for q in range(4):
            cols = slice(q * quarter + at * 128, q * quarter + (at + 2) * 128)
            back = jnp.dot(both, w_all[: 2 * PAD, cols], preferred_element_type=f32)
            wide[at, pl.ds(q, count, stride=4), :] = back[:, :128]
            wide[at + 1, pl.ds(q, count, stride=4), :] = back[:, 128:]
        for i in (at, at + 1):
            part_ref[:, i * tall : (i + 1) * tall, :] = wide[i].reshape(peers, tall, 128).astype(bf16)


def score_pieces(score):
    lane = lax.broadcasted_iota(jnp.int32, (score.shape[0], 128), 1)
    rest = jnp.broadcast_to(score, lane.shape)
    out = jnp.zeros_like(rest)
    for i in range(3):
        piece = rest.astype(bf16).astype(f32)
        out = jnp.where(lane == i, piece, out)
        rest = rest - piece
    return out


def summed(got_ref):
    acc = got_ref[0].astype(f32)
    for i in range(1, got_ref.shape[0]):
        acc = acc + got_ref[i].astype(f32)
    return acc


def middle_kernel(got_ref, part_hbm, part_ref, tile, scores, sem):
    peers = part_ref.shape[0]
    tall = peers * 8
    acc = summed(got_ref)
    blocks = (acc.shape[0] - tall // 4) // tall
    for i in range(blocks):
        rows = acc[i * tall : (i + 1) * tall].reshape(peers, 8, 128)
        part_ref[:, i * 8 : (i + 1) * 8, :] = rows.astype(bf16)
    scores[...] = score_pieces(jnp.sum(acc[blocks * tall :], axis=1, keepdims=True))
    tile[...] = jnp.zeros_like(tile)
    for a in range(peers):
        tile[a, 0:CAP] = scores[CAP * a : CAP * (a + 1)]
    part_ref[:, blocks * 8 :, :] = tile[...].astype(bf16)
    copy = pltpu.make_async_copy(part_ref, part_hbm, sem)
    copy.start()
    copy.wait()


def last_kernel(got_ref, cot_ref, w_ref, t_ref, held_ref, moved_ref, grad_ref):
    acc = summed(got_ref)
    quarter = cot_ref.shape[1]
    w = w_ref[...]
    for i in range(quarter // 128):
        cols = slice(i * 128, (i + 1) * 128)
        back = acc[i * 8 : (i + 1) * 8].astype(bf16).astype(f32)
        moved_ref[:, cols] = (cot_ref[:, cols] + w * back).astype(bf16)
    moved_ref[:, quarter:] = t_ref[...].astype(bf16)
    score = jnp.sum(acc[quarter // 16 :], axis=1, keepdims=True)
    grad_ref[...] = held_ref[0:2] * score[0:1] + held_ref[4:6] * score[1:2]


def place_kernel(cot_ref, moved_ref, out_ref, ready, sems):
    tokens, width = cot_ref.shape
    quarter = width // 4
    row = lax.broadcasted_iota(jnp.int32, (tokens, 128), 0).astype(f32)
    token = moved_ref[:, quarter:].astype(f32)
    at = [(row == token[4 * s : 4 * s + 1])[:, :1] for s in range(CAP)]
    copies = []
    for q in range(4):
        cols = slice(q * quarter, (q + 1) * quarter)
        value = cot_ref[:, cols].astype(f32)
        for s in range(CAP):
            value = jnp.where(at[s], moved_ref[4 * s + q : 4 * s + q + 1, :quarter].astype(f32), value)
        ready[:, cols] = value.astype(bf16)
        copies.append(pltpu.make_async_copy(ready.at[:, cols], out_ref.at[:, cols], sems.at[q]))
        copies[q].start()
    for copy in copies:
        copy.wait()


def call(kernel, outs, *operands, scratch=(), smem=(), near=(), far=(), out_space=pltpu.VMEM):
    def placed(i, v):
        if i in near or i in far:
            return pltpu.with_memory_space_constraint(v, pltpu.VMEM if i in near else pltpu.HBM)
        return v

    def space(i):
        return pltpu.SMEM if i in smem else pltpu.HBM if i in far else pltpu.VMEM

    return pl.pallas_call(
        kernel,
        out_shape=outs,
        in_specs=[pl.BlockSpec(memory_space=space(i)) for i in range(len(operands))],
        out_specs=[pl.BlockSpec(memory_space=out_space)] * len(outs),
        scratch_shapes=list(scratch),
        compiler_params=pltpu.CompilerParams(vmem_limit_bytes=24 << 20),
    )(*(placed(i, v) for i, v in enumerate(operands)))


def shape(dims, kind):
    return jax.ShapeDtypeStruct(dims, kind)


def on_device(layer_input, cotangent, route_weight, chosen, hot_expert, store_in, store_out):
    tokens, width = layer_input.shape[1:]
    half, quarter = width // 2, width // 4
    num_row = lax.axis_size("row")
    heights = num_row // PLANE
    peers = heights // 2
    along_z = [[a * 2 * PLANE + r for a in range(peers)] for r in range(2 * PLANE)]
    in_plane = [[z * PLANE + i for i in range(PLANE)] for z in range(heights)]
    sections = lax.axis_size("section")
    back_one = [(i, i - 1) for i in range(1, sections)]

    def exchange(value, groups):
        return lax.all_to_all(
            value, "row", split_axis=0, concat_axis=0, axis_index_groups=groups, tiled=True
        )

    def along(value, by):
        return lax.ppermute(value, "row", [(i, (i + by * PLANE) % num_row) for i in range(num_row)])

    w_in = jnp.swapaxes(store_in[0], 1, 2)
    w_out = store_out[0]
    w_both = jnp.concatenate([w_in, w_out[None]], axis=0)
    from_above = along(w_both[:, :SENT_DOWN], -1)
    from_below = along(w_both[:, SENT_DOWN:], 1)
    cot_moved = lax.ppermute(cotangent[0], "section", back_one)

    unit, cot_rows, w_rows, t_rows, held = call(
        select_kernel,
        [
            pltpu.VMEM((peers, 8, half), bf16),
            pltpu.VMEM((8, quarter), f32),
            pltpu.VMEM((8, tokens), f32),
            pltpu.VMEM((8, tokens), f32),
            pltpu.VMEM((8, tokens), f32),
        ],
        chosen[0].T,
        hot_expert,
        route_weight[0].T,
        layer_input[0],
        cotangent[0],
        (lax.axis_index("section") % 2 * TURNS).reshape(1),
        scratch=(
            pltpu.VMEM((TOP, tokens), jnp.int32),
            pltpu.VMEM((TOP, tokens), f32),
            pltpu.VMEM((tokens, width), bf16),
            pltpu.VMEM((tokens, width), bf16),
            pltpu.VMEM((8, 128), f32),
            pltpu.SemaphoreType.DMA((4,)),
        ),
        smem=(1, 5),
        far=(0, 2, 3, 4),
    )
    tall = peers * 8
    column = exchange(unit, along_z).reshape(tall, half)
    (sent,) = call(
        spread_kernel,
        [pltpu.HBM((PLANE, tall, half), bf16)],
        column,
        scratch=(pltpu.SemaphoreType.DMA((PLANE,)),),
        near=(0,),
        out_space=pltpu.HBM,
    )
    rows = exchange(sent, in_plane)
    (w_all,) = call(
        weights_kernel,
        [pltpu.VMEM((3 * PAD, width), bf16)],
        w_in,
        w_out,
        from_below,
        from_above,
        near=(0, 1, 2, 3),
    )
    count = PLANE * tall
    (part,) = call(
        expert_kernel,
        [pltpu.VMEM((PLANE, quarter // 128 * tall + tall // 4, 128), bf16)],
        rows.reshape(count, half),
        w_all,
        scratch=(
            pltpu.VMEM((count, half), bf16),
            pltpu.VMEM((6, count, PAD), f32),
            pltpu.VMEM((quarter // 128, count, 128), f32),
            pltpu.SemaphoreType.DMA,
        ),
        near=(1,),
        far=(0,),
    )
    got = exchange(part, in_plane)
    part_shape = (peers, quarter // 16 + 8, 128)
    (part,) = call(
        middle_kernel,
        [pltpu.HBM(part_shape, bf16)],
        got,
        scratch=(
            pltpu.VMEM(part_shape, bf16),
            pltpu.VMEM((peers, 8, 128), f32),
            pltpu.VMEM((peers * CAP, 128), f32),
            pltpu.SemaphoreType.DMA,
        ),
        near=(0,),
        out_space=pltpu.HBM,
    )
    got = exchange(part, along_z)
    moved, grad = call(
        last_kernel,
        [pltpu.VMEM((8, quarter + 128), bf16), shape((TOP, tokens), f32)],
        got,
        cot_rows,
        w_rows,
        t_rows,
        held,
        near=(0, 1, 2, 3, 4),
    )
    moved = lax.ppermute(moved, "section", back_one)
    (back_cot,) = call(
        place_kernel,
        [pltpu.HBM((tokens, width), bf16)],
        cot_moved,
        moved,
        scratch=(pltpu.VMEM((tokens, width), bf16), pltpu.SemaphoreType.DMA((4,))),
        near=(0, 1),
        out_space=pltpu.HBM,
    )
    return (back_cot[None], grad.T[None])


def solution(mesh):
    in_specs = (
        P("section", "row", None),
        P("section", "row", None),
        P("section", "row", None),
        P("section", "row", None),
        P("section"),
        P("section", None, None, "row"),
        P("section", "row", None),
    )
    out_specs = (P("section", "row", None), P("section", "row", None))

    return jax.shard_map(on_device, mesh=mesh, in_specs=in_specs, out_specs=out_specs, check_vma=False)
```

```python
import jax
import jax.numpy as jnp
from jax import lax
from jax.experimental import pallas as pl
from jax.experimental.pallas import tpu as pltpu
from jax.sharding import PartitionSpec as P


CAP = 2
TOP = 2
TURNS = 2200
PLANE = 8
SENT_DOWN = 32
PAD = 128
NONE = 128

bf16 = jnp.bfloat16
f32 = jnp.float32


def slot_tokens(chosen, hot):
    hit = chosen == hot
    lane = lax.broadcasted_iota(jnp.int32, hit.shape, 1)
    at = jnp.where(hit, lane, NONE)
    first = jnp.min(jnp.min(at, axis=1, keepdims=True), axis=0, keepdims=True)
    later = jnp.where(at > first, at, NONE)
    second = jnp.min(jnp.min(later, axis=1, keepdims=True), axis=0, keepdims=True)
    return hit, lane, first, second


def total(values):
    return jnp.sum(jnp.sum(values, axis=1, keepdims=True), axis=0, keepdims=True)


def select_kernel(
    chosen_hbm, hot_ref, weight_hbm, x_hbm, g_hbm, turns_ref,
    sent_ref, cot_ref, w_ref, t_ref, held_ref,
    chosen_ref, weight_ref, x_ref, g_ref, spun_ref, sems,
):
    pairs = (
        (chosen_hbm, chosen_ref),
        (weight_hbm, weight_ref),
        (x_hbm, x_ref),
        (g_hbm, g_ref),
    )
    coming = [pltpu.make_async_copy(src, dst, sems.at[i]) for i, (src, dst) in enumerate(pairs)]
    for copy in coming:
        copy.start()
    for copy in coming[:2]:
        copy.wait()
    hit, lane, first, second = slot_tokens(chosen_ref[...], hot_ref[0])
    weights = weight_ref[...]
    in_first, in_second = hit & (lane == first), hit & (lane == second)
    held_ref[...] = jnp.zeros_like(held_ref)
    held_ref[0:2] = in_first.astype(f32)
    held_ref[4:6] = in_second.astype(f32)
    w_first = total(jnp.where(in_first, weights, 0.0))
    w_second = total(jnp.where(in_second, weights, 0.0))
    tokens = x_ref.shape[0]
    row = lax.broadcasted_iota(jnp.int32, (8, tokens), 0)
    col = lax.broadcasted_iota(jnp.int32, (8, tokens), 1)
    token = jnp.where(row < 4, first, second)
    pick = (col == token).astype(f32).astype(bf16)
    t_ref[...] = token.astype(f32)
    w_ref[...] = jnp.where(row < 4, w_first, w_second)
    for copy in coming[2:]:
        copy.wait()
    x_rows = jnp.dot(pick, x_ref[...], preferred_element_type=f32)
    g_rows = jnp.dot(pick, g_ref[...], preferred_element_type=f32)
    half = x_rows.shape[1] // 2
    quarter = half // 2
    at = lax.broadcasted_iota(jnp.int32, (8, half), 0)
    low = (at & 2) == 0
    unit = jnp.where(
        (at & 1) == 0,
        jnp.where(low, x_rows[:, :half], x_rows[:, half:]),
        jnp.where(low, g_rows[:, :half], g_rows[:, half:]),
    ).astype(bf16)
    for i in range(sent_ref.shape[0]):
        sent_ref[i] = unit

    def turn(i, carry):
        spun_ref[...] = spun_ref[...] + 1.0
        return carry

    spun_ref[...] = jnp.zeros_like(spun_ref)
    lax.fori_loop(0, turns_ref[0], turn, 0)
    at = lax.broadcasted_iota(jnp.int32, (8, quarter), 0) & 3
    cot = g_rows[:, :quarter]
    for q in range(1, 4):
        cot = jnp.where(at == q, g_rows[:, q * quarter : (q + 1) * quarter], cot)
    cot_ref[...] = cot


def weights_kernel(in_ref, out_ref, below_ref, above_ref, w_all):
    width, own = in_ref.shape[2], in_ref.shape[1]
    n_above, n_below = above_ref.shape[1], below_ref.shape[1]
    for kind in range(3):
        at = kind * PAD
        w_all[at + 48 : at + 64, :] = jnp.zeros((16, width), bf16)
        w_all[at + 112 : at + 128, :] = jnp.zeros((16, width), bf16)
        w_all[at : at + n_above, :] = above_ref[kind]
        w_all[at + n_above : at + n_above + n_below, :] = below_ref[kind]
        w_all[at + 64 : at + 64 + own, :] = in_ref[kind] if kind < 2 else out_ref[...]


def spread_kernel(column_ref, sent_ref, sems):
    peers, part = sent_ref.shape[0], sent_ref.shape[1] // 2
    copies = [
        pltpu.make_async_copy(
            column_ref.at[h * part : (h + 1) * part],
            sent_ref.at[i, h * part : (h + 1) * part],
            sems.at[2 * i + h],
        )
        for i in range(peers)
        for h in range(2)
    ]
    for copy in copies:
        copy.start()
    for copy in copies:
        copy.wait()


def expert_kernel(rows_hbm, w_all, part_ref, rows_ref, prod, wide, sem):
    width = w_all.shape[1]
    half, quarter = width // 2, width // 4
    count = rows_ref.shape[0] // 4
    part = rows_ref.shape[0] // 8
    coming = [
        pltpu.make_async_copy(
            rows_hbm.at[i * part : (i + 1) * part], rows_ref.at[i * part : (i + 1) * part], sem.at[i]
        )
        for i in range(8)
    ]
    for copy in coming:
        copy.start()
    for copy in coming:
        copy.wait()
    nt = (((1,), (1,)), ((), ()))
    for h in range(2):
        cols = slice(h * half, (h + 1) * half)
        out = lax.dot_general(rows_ref[...], w_all[:, cols], nt, preferred_element_type=f32)
        for column in range(3):
            prod[h * 3 + column] = out[:, column * PAD : (column + 1) * PAD]

    def taken(kind, column):
        low = prod[column, pl.ds(kind, count, stride=4), :]
        return low + prod[3 + column, pl.ds(2 + kind, count, stride=4), :]

    gate, upper, d_hidden = taken(0, 0), taken(0, 1), taken(1, 2)
    sig = 1.0 / (1.0 + jnp.exp(-gate))
    hidden = (gate * sig * upper).astype(bf16)
    d_gate = (d_hidden * upper * sig * (1.0 + gate * (1.0 - sig))).astype(bf16)
    d_up = (d_hidden * gate * sig).astype(bf16)
    score = jnp.sum(hidden.astype(f32) * d_hidden, axis=1, keepdims=True)
    both = jnp.concatenate([d_gate, d_up], axis=1)
    peers, tall = part_ref.shape[0], rows_ref.shape[0] // part_ref.shape[0]
    blocks = quarter // 128
    part_ref[:, blocks * tall :, :] = score_pieces(score).reshape(peers, tall // 4, 128).astype(bf16)
    for at in range(0, blocks, 2):
        for q in range(4):
            cols = slice(q * quarter + at * 128, q * quarter + (at + 2) * 128)
            back = jnp.dot(both, w_all[: 2 * PAD, cols], preferred_element_type=f32)
            wide[at, pl.ds(q, count, stride=4), :] = back[:, :128]
            wide[at + 1, pl.ds(q, count, stride=4), :] = back[:, 128:]
        for i in (at, at + 1):
            part_ref[:, i * tall : (i + 1) * tall, :] = wide[i].reshape(peers, tall, 128).astype(bf16)


def score_pieces(score):
    lane = lax.broadcasted_iota(jnp.int32, (score.shape[0], 128), 1)
    rest = jnp.broadcast_to(score, lane.shape)
    out = jnp.zeros_like(rest)
    for i in range(3):
        piece = rest.astype(bf16).astype(f32)
        out = jnp.where(lane == i, piece, out)
        rest = rest - piece
    return out


def summed(got_ref):
    acc = got_ref[0].astype(f32)
    for i in range(1, got_ref.shape[0]):
        acc = acc + got_ref[i].astype(f32)
    return acc


def middle_kernel(got_ref, part_hbm, part_ref, tile, scores, sem):
    peers = part_ref.shape[0]
    tall = peers * 8
    acc = summed(got_ref)
    blocks = (acc.shape[0] - tall // 4) // tall
    for i in range(blocks):
        rows = acc[i * tall : (i + 1) * tall].reshape(peers, 8, 128)
        part_ref[:, i * 8 : (i + 1) * 8, :] = rows.astype(bf16)
    scores[...] = score_pieces(jnp.sum(acc[blocks * tall :], axis=1, keepdims=True))
    tile[...] = jnp.zeros_like(tile)
    for a in range(peers):
        tile[a, 0:CAP] = scores[CAP * a : CAP * (a + 1)]
    part_ref[:, blocks * 8 :, :] = tile[...].astype(bf16)
    copy = pltpu.make_async_copy(part_ref, part_hbm, sem)
    copy.start()
    copy.wait()


def last_kernel(got_ref, cot_ref, w_ref, t_ref, held_ref, moved_ref, grad_ref):
    acc = summed(got_ref)
    quarter = cot_ref.shape[1]
    w = w_ref[...]
    for i in range(quarter // 128):
        cols = slice(i * 128, (i + 1) * 128)
        back = acc[i * 8 : (i + 1) * 8].astype(bf16).astype(f32)
        moved_ref[:, cols] = (cot_ref[:, cols] + w * back).astype(bf16)
    moved_ref[:, quarter:] = t_ref[...].astype(bf16)
    score = jnp.sum(acc[quarter // 16 :], axis=1, keepdims=True)
    grad_ref[...] = held_ref[0:2] * score[0:1] + held_ref[4:6] * score[1:2]


def place_kernel(cot_ref, moved_ref, out_ref, ready, sems):
    tokens, width = cot_ref.shape
    quarter = width // 4
    row = lax.broadcasted_iota(jnp.int32, (tokens, 128), 0).astype(f32)
    token = moved_ref[:, quarter:].astype(f32)
    at = [(row == token[4 * s : 4 * s + 1])[:, :1] for s in range(CAP)]
    copies = []
    for q in range(4):
        cols = slice(q * quarter, (q + 1) * quarter)
        value = cot_ref[:, cols].astype(f32)
        for s in range(CAP):
            value = jnp.where(at[s], moved_ref[4 * s + q : 4 * s + q + 1, :quarter].astype(f32), value)
        ready[:, cols] = value.astype(bf16)
        copies.append(pltpu.make_async_copy(ready.at[:, cols], out_ref.at[:, cols], sems.at[q]))
        copies[q].start()
    for copy in copies:
        copy.wait()


def call(kernel, outs, *operands, scratch=(), smem=(), near=(), far=(), out_space=pltpu.VMEM):
    def placed(i, v):
        if i in near or i in far:
            return pltpu.with_memory_space_constraint(v, pltpu.VMEM if i in near else pltpu.HBM)
        return v

    def space(i):
        return pltpu.SMEM if i in smem else pltpu.HBM if i in far else pltpu.VMEM

    return pl.pallas_call(
        kernel,
        out_shape=outs,
        in_specs=[pl.BlockSpec(memory_space=space(i)) for i in range(len(operands))],
        out_specs=[pl.BlockSpec(memory_space=out_space)] * len(outs),
        scratch_shapes=list(scratch),
        compiler_params=pltpu.CompilerParams(vmem_limit_bytes=24 << 20),
    )(*(placed(i, v) for i, v in enumerate(operands)))


def shape(dims, kind):
    return jax.ShapeDtypeStruct(dims, kind)


def on_device(layer_input, cotangent, route_weight, chosen, hot_expert, store_in, store_out):
    tokens, width = layer_input.shape[1:]
    half, quarter = width // 2, width // 4
    num_row = lax.axis_size("row")
    heights = num_row // PLANE
    peers = heights // 2
    along_z = [[a * 2 * PLANE + r for a in range(peers)] for r in range(2 * PLANE)]
    in_plane = [[z * PLANE + i for i in range(PLANE)] for z in range(heights)]
    sections = lax.axis_size("section")
    back_one = [(i, i - 1) for i in range(1, sections)]

    def exchange(value, groups):
        return lax.all_to_all(
            value, "row", split_axis=0, concat_axis=0, axis_index_groups=groups, tiled=True
        )

    def along(value, by):
        return lax.ppermute(value, "row", [(i, (i + by * PLANE) % num_row) for i in range(num_row)])

    w_in = jnp.swapaxes(store_in[0], 1, 2)
    w_out = store_out[0]
    w_both = jnp.concatenate([w_in, w_out[None]], axis=0)
    from_above = along(w_both[:, :SENT_DOWN], -1)
    from_below = along(w_both[:, SENT_DOWN:], 1)
    cot_moved = lax.ppermute(cotangent[0], "section", back_one)

    unit, cot_rows, w_rows, t_rows, held = call(
        select_kernel,
        [
            pltpu.VMEM((peers, 8, half), bf16),
            pltpu.VMEM((8, quarter), f32),
            pltpu.VMEM((8, tokens), f32),
            pltpu.VMEM((8, tokens), f32),
            pltpu.VMEM((8, tokens), f32),
        ],
        chosen[0].T,
        hot_expert,
        route_weight[0].T,
        layer_input[0],
        cotangent[0],
        (lax.axis_index("section") % 2 * TURNS).reshape(1),
        scratch=(
            pltpu.VMEM((TOP, tokens), jnp.int32),
            pltpu.VMEM((TOP, tokens), f32),
            pltpu.VMEM((tokens, width), bf16),
            pltpu.VMEM((tokens, width), bf16),
            pltpu.VMEM((8, 128), f32),
            pltpu.SemaphoreType.DMA((4,)),
        ),
        smem=(1, 5),
        far=(0, 2, 3, 4),
    )
    tall = peers * 8
    column = exchange(unit, along_z).reshape(tall, half)
    (sent,) = call(
        spread_kernel,
        [pltpu.HBM((PLANE, tall, half), bf16)],
        column,
        scratch=(pltpu.SemaphoreType.DMA((2 * PLANE,)),),
        near=(0,),
        out_space=pltpu.HBM,
    )
    rows = exchange(sent, in_plane)
    (w_all,) = call(
        weights_kernel,
        [pltpu.VMEM((3 * PAD, width), bf16)],
        w_in,
        w_out,
        from_below,
        from_above,
        near=(0, 1, 2, 3),
    )
    count = PLANE * tall
    (part,) = call(
        expert_kernel,
        [pltpu.VMEM((PLANE, quarter // 128 * tall + tall // 4, 128), bf16)],
        rows.reshape(count, half),
        w_all,
        scratch=(
            pltpu.VMEM((count, half), bf16),
            pltpu.VMEM((6, count, PAD), f32),
            pltpu.VMEM((quarter // 128, count, 128), f32),
            pltpu.SemaphoreType.DMA((8,)),
        ),
        near=(1,),
        far=(0,),
    )
    got = exchange(part, in_plane)
    part_shape = (peers, quarter // 16 + 8, 128)
    (part,) = call(
        middle_kernel,
        [pltpu.HBM(part_shape, bf16)],
        got,
        scratch=(
            pltpu.VMEM(part_shape, bf16),
            pltpu.VMEM((peers, 8, 128), f32),
            pltpu.VMEM((peers * CAP, 128), f32),
            pltpu.SemaphoreType.DMA,
        ),
        near=(0,),
        out_space=pltpu.HBM,
    )
    got = exchange(part, along_z)
    moved, grad = call(
        last_kernel,
        [pltpu.VMEM((8, quarter + 128), bf16), shape((TOP, tokens), f32)],
        got,
        cot_rows,
        w_rows,
        t_rows,
        held,
        near=(0, 1, 2, 3, 4),
    )
    moved = lax.ppermute(moved, "section", back_one)
    (back_cot,) = call(
        place_kernel,
        [pltpu.HBM((tokens, width), bf16)],
        cot_moved,
        moved,
        scratch=(pltpu.VMEM((tokens, width), bf16), pltpu.SemaphoreType.DMA((4,))),
        near=(0, 1),
        out_space=pltpu.HBM,
    )
    return (back_cot[None], grad.T[None])


def solution(mesh):
    in_specs = (
        P("section", "row", None),
        P("section", "row", None),
        P("section", "row", None),
        P("section", "row", None),
        P("section"),
        P("section", None, None, "row"),
        P("section", "row", None),
    )
    out_specs = (P("section", "row", None), P("section", "row", None))

    return jax.shard_map(on_device, mesh=mesh, in_specs=in_specs, out_specs=out_specs, check_vma=False)
```
